32 devices in a mesh: groups: 2 (over y), seq: 4 (over z), head: 2 (over x), sub: 2 (over core).
Axes of the slice: x: 2, y: 2, z: 4, core: 2. Of those that a mesh axis runs over, the one named last changes fastest.
Arguments:
- x_raw: bfloat16 [16, 128, 8192], P(('groups', 'seq', 'sub'), 'head'), parts along dimension 0, may hold values from -6 to 6
- bc_raw: bfloat16 [16, 128, 2048], P(('groups', 'seq', 'sub'), 'head'), parts along dimension 0, may hold values from -6 to 6
- dt_raw: bfloat16 [16, 128, 128], P(('groups', 'seq', 'sub'), 'head'), parts along dimension 0, may hold values from -3 to 40
- conv_x_weight: float32 [4, 8192], P(None, 'head'), may hold values from -3 to 3
- conv_x_bias: float32 [8192], P('head'), may hold values from -2.5 to 2.5
- conv_bc_weight: float32 [4, 2048], P(None, 'head'), may hold values from -3 to 3
- conv_bc_bias: float32 [2048], P('head'), may hold values from -2.5 to 2.5
- stride_offset_per_head: float32 [128], P('head'), may hold values from -12 to 0
- a_log: float32 [128], P('head'), may hold values from -8 to 3
- skip_d: float32 [128], P('head'), may hold values from 0.5 to 1.5
- norm_gain: float32 [8192], P('head'), may hold values from 0.1 to 1.9
Outputs:
- mixed: bfloat16 [16, 128, 8192], P(('groups', 'seq', 'sub'), None, 'head'), parts along dimension 0
The draws below stay inside these ranges and needn't reach their ends.
There are 2 independent parts, one for each index of `groups`. The reference program is written for one: setup_inputs(seed, part) draws one part's arguments, and reference() takes and returns one part's arrays. A program takes and returns all parts, laid end to end along the dimension named above; an argument that names none is the same for every part. Nothing has to cross between parts.
All inputs are finite; a program needn't handle non-finite values.
Results may differ from the reference program's by a relative error of at most 0.0061.
Values may be sent and summed in bfloat16 or wider, within the bound.
No kernel may reach another device: no remote copies, remote signals or barrier semaphores. Data moves between devices by JAX's collectives and lax.ppermute only.
A program may use at most 128 MiB of HBM per device.

```python
import math
import jax
import jax.numpy as jnp
from jax import lax

HEADS = 128
HEAD_DIM = 64
STATE = 128
GROUPS = 8
CONV = 4
SPAN = 128
ROWS = 128
NBLOCKS = 8
SPELL_LENGTH = 1024
INNER = 8192


def head_table(key):
    seed_sequence = jax.random.split(jax.random.fold_in(key, 11), 4)
    fast_count = HEADS // 2
    order = jax.random.permutation(seed_sequence[0], HEADS)
    is_fast = order < fast_count
    slow_rate = jax.random.uniform(seed_sequence[1], (HEADS,), jnp.float32, 0.25, 0.45) * math.log(10.0) / SPELL_LENGTH
    fast_rate = 1.0 / jax.random.uniform(seed_sequence[2], (HEADS,), jnp.float32, 30.0, 50.0)
    decay_rate = jnp.where(is_fast, fast_rate, slow_rate)
    stored_values = jnp.minimum(1.0 / decay_rate, float(SPELL_LENGTH))
    spread = jnp.exp(jax.random.uniform(seed_sequence[3], (HEADS,), jnp.float32, -0.35, 0.35))
    step_size = spread / jnp.sqrt(STATE * stored_values)
    return (jnp.log(decay_rate / step_size), jnp.log(jnp.expm1(step_size)))


def draw_a_log(key, part):
    return head_table(key)[0]


def draw_stride_offset_per_head(key, part):
    return head_table(key)[1]


def draw_dt_raw(key, part):
    seed_sequence = jax.random.split(jax.random.fold_in(key, 23), 3)
    jitter = jax.random.uniform(seed_sequence[0], (NBLOCKS, ROWS, HEADS), jnp.float32, -0.7, 0.7)
    displacement = jax.random.uniform(seed_sequence[1], (NBLOCKS, 1, 1), jnp.float32, -0.5, 0.5)
    spell_index = jax.random.randint(seed_sequence[2], (3,), 0, SPELL_LENGTH)
    sequence_place = jnp.arange(NBLOCKS)[:, None] * ROWS + jnp.arange(ROWS)[None, :]
    marked_indicator = jnp.any(sequence_place[:, :, None] == spell_index[None, None, :], axis=2)
    lift_size = 0.5 * math.log(STATE * SPELL_LENGTH) + 0.43 * math.sqrt(SPELL_LENGTH / STATE)
    return (jitter + displacement + jnp.where(marked_indicator[:, :, None], lift_size, 0.0)).astype(jnp.bfloat16)


def shard_levels(own_key, extent, cuts, least, largest):
    loudness = 1.0
    for axis_at, parts in cuts:
        steps = jax.random.uniform(jax.random.fold_in(jax.random.fold_in(own_key, 6), axis_at), (parts,), jnp.float32, least / len(cuts), largest / len(cuts))
        loudness = loudness * jnp.repeat(jnp.exp(steps), extent[axis_at] // parts).reshape((-1,) + (1,) * (len(extent) - 1 - axis_at))
    return loudness


def noise(rng, dims, deviation, reach, cuts=(), kind=jnp.bfloat16):
    values = jax.random.normal(rng, dims, jnp.float32) * deviation
    if len(cuts) > 0:
        values = shard_levels(rng, dims, cuts, -0.22, 0.18) * values
    return jnp.clip(values, min=-reach, max=reach).astype(kind)


def setup_inputs(seed: int = 0, part: int = 0) -> dict:
    streams_of = jax.random.split(jax.random.key(seed), 12)
    own_keys = jax.random.split(jax.random.fold_in(streams_of[11], part), 12)
    return {
        "x_raw": noise(own_keys[0], (NBLOCKS, ROWS, INNER), 1.0, 6.0, ((0, 8), (1, 2))),
        "bc_raw": noise(own_keys[1], (NBLOCKS, ROWS, 2 * GROUPS * STATE), 1.0, 6.0, ((0, 8), (1, 2))),
        "dt_raw": draw_dt_raw(jax.random.fold_in(jax.random.fold_in(streams_of[11], part), 71), part),
        "conv_x_weight": noise(streams_of[3], (CONV, INNER), CONV ** -0.5, 3.0, ((1, 2),), jnp.float32),
        "conv_x_bias": noise(streams_of[4], (INNER,), 0.3, 2.5, ((0, 2),), jnp.float32),
        "conv_bc_weight": noise(streams_of[5], (CONV, 2 * GROUPS * STATE), CONV ** -0.5, 3.0, ((1, 2),), jnp.float32),
        "conv_bc_bias": noise(streams_of[6], (2 * GROUPS * STATE,), 0.3, 2.5, ((0, 2),), jnp.float32),
        "stride_offset_per_head": draw_stride_offset_per_head(jax.random.fold_in(streams_of[11], 71), part),
        "a_log": draw_a_log(jax.random.fold_in(streams_of[11], 71), part),
        "skip_d": jnp.clip(0.5 + 1.0 * jax.random.uniform(streams_of[9], (HEADS,), jnp.float32) ** shard_levels(streams_of[9], (HEADS,), ((0, 2),), -0.2, 0.2), 0.5, 1.5),
        "norm_gain": jnp.clip(1.0 + 0.18 * jax.random.normal(streams_of[10], (INNER,), jnp.float32), 0.1, 1.9),
    }


NORM_EPSILON = 1e-05

def rounded(values):
    return lax.optimization_barrier(values.astype(jnp.bfloat16)).astype(jnp.float32)

def conv_rows(raw_rows, rim_rows, weight, bias):
    conv_width = weight.shape[0]
    row_count = raw_rows.shape[0]
    joined = jnp.concatenate([rim_rows, raw_rows], axis=0).astype(jnp.float32)
    running = bias[None, :]
    for tap_index in range(conv_width):
        running = running + weight[tap_index][None, :] * joined[tap_index:tap_index + row_count]
    return jax.nn.silu(running).astype(jnp.bfloat16)

def reference(x_raw, bc_raw, dt_raw, conv_x_weight, conv_x_bias, conv_bc_weight, conv_bc_bias, stride_offset_per_head, a_log, skip_d, norm_gain):
    blocks = SPELL_LENGTH // SPAN
    per_group = HEADS // GROUPS
    x_all = x_raw.reshape(blocks, SPAN, INNER)
    bc_all = bc_raw.reshape(blocks, SPAN, 2 * GROUPS * STATE)
    dt_all = dt_raw.reshape(blocks, SPAN, HEADS)
    causal = lax.broadcasted_iota(jnp.int32, (SPAN, SPAN), 0) >= lax.broadcasted_iota(jnp.int32, (SPAN, SPAN), 1)
    decay_rate = -jnp.exp(a_log)

    def one_block(running, block_item):
        carried_state, x_tail, bc_tail = running
        x_rows, bc_rows, dt_rows = block_item
        x_conv = conv_rows(x_rows, x_tail, conv_x_weight, conv_x_bias)
        bc_conv = conv_rows(bc_rows, bc_tail, conv_bc_weight, conv_bc_bias)
        dt_step = jax.nn.softplus(dt_rows.astype(jnp.float32) + stride_offset_per_head[None, :])
        cum_decay = jnp.cumsum(decay_rate[None, :] * dt_step, axis=0)
        x_heads = lax.optimization_barrier(x_conv).astype(jnp.float32).reshape(SPAN, GROUPS, per_group, HEAD_DIM)
        bc_heads = lax.optimization_barrier(bc_conv).astype(jnp.float32).reshape(SPAN, GROUPS, 2, STATE)
        b_in = bc_heads[:, :, 0]
        c_out = bc_heads[:, :, 1]
        inner_prod = jnp.einsum('tgn,sgn->gts', c_out, b_in)
        cum_heads = cum_decay.T.reshape(GROUPS, per_group, SPAN)
        step_heads = dt_step.T.reshape(GROUPS, per_group, SPAN)
        gap_pairs = cum_heads[..., :, None] - cum_heads[..., None, :]
        weight = jnp.exp(jnp.where(causal, gap_pairs, -1e+30)) * step_heads[..., None, :]
        mixing = rounded(inner_prod[:, None] * weight)
        within_block_output = jnp.einsum('gjts,sgjp->tgjp', mixing, x_heads)
        block_end = cum_decay[-1]
        to_end = jnp.exp(block_end[None, :] - cum_decay) * dt_step
        scaled = rounded(to_end.reshape(SPAN, GROUPS, per_group, 1) * x_heads)
        block_state = jnp.einsum('sgjp,sgn->gjpn', scaled, b_in)
        carried_bf = rounded(carried_state)
        y_state = jnp.einsum('tgn,gjpn->tgjp', c_out, carried_bf) * jnp.exp(cum_decay).reshape(SPAN, GROUPS, per_group, 1)
        complete_output = within_block_output + y_state + skip_d.reshape(GROUPS, per_group, 1) * x_heads
        squares_mean = lax.optimization_barrier(jnp.mean(complete_output * complete_output, axis=(2, 3)))
        normed = complete_output * lax.rsqrt(squares_mean + NORM_EPSILON)[:, :, None, None] * norm_gain.reshape(GROUPS, per_group, HEAD_DIM)
        new_state = jnp.exp(block_end).reshape(GROUPS, per_group, 1, 1) * carried_state + block_state
        tails = (x_rows[SPAN - CONV + 1:], bc_rows[SPAN - CONV + 1:])
        return ((new_state, tails[0], tails[1]), normed.reshape(SPAN, INNER).astype(jnp.bfloat16))
    start = (jnp.zeros((GROUPS, per_group, HEAD_DIM, STATE), jnp.float32), jnp.zeros((CONV - 1, INNER), x_raw.dtype), jnp.zeros((CONV - 1, 2 * GROUPS * STATE), bc_raw.dtype))
    final_carry, outputs = lax.scan(one_block, start, (x_all, bc_all, dt_all))
    return outputs.reshape(NBLOCKS, ROWS, INNER)
```

```python
import functools

import jax
import jax.numpy as jnp
from jax import lax
from jax.experimental import pallas as pl
from jax.experimental.pallas import tpu as pltpu
from jax.sharding import PartitionSpec as P

STATE = 128
SPAN = 128
LANES = 128
EDGE = 8
EXTRA = 16
NORM_EPSILON = 1e-05
CHUNKS = 2


F32 = jnp.float32
BF16 = jnp.bfloat16


def silu(v):
    return v / (1.0 + jnp.exp(-v))


def widen_pair(table, head, head_dim, lanes):
    count = LANES // head_dim
    strip = jnp.broadcast_to(table[:, head : head + 1], (table.shape[0], LANES))
    for k in range(1, count):
        column = jnp.broadcast_to(table[:, head + k : head + k + 1], (table.shape[0], LANES))
        strip = jnp.where(lanes >= k * head_dim, column, strip)
    return strip


def lane_index(rows):
    return lax.broadcasted_iota(jnp.int32, (rows, LANES), 1)


def tables_kernel(heads, place, own_ref, *refs):
    *recv_refs, offset_ref, a_log_ref, tok_ref, head_ref, raw = refs
    position = place[0]
    rows = own_ref.shape[1]
    shards = len(recv_refs) + 1
    raw[pl.ds(pl.multiple_of(position * rows, rows), rows), :] = own_ref[0].astype(F32)
    for k, ref in enumerate(recv_refs):
        source = lax.rem(position + shards - 1 - k, shards)
        raw[pl.ds(pl.multiple_of(source * rows, rows), rows), :] = ref[...].astype(F32)
    logits = raw[...]
    if shards > 1:
        total = logits.shape[1]
        logits = pltpu.roll(logits, lax.rem(total - position * heads, total), axis=1)
    v = logits[:, :heads] + offset_ref[...]
    dt = jnp.maximum(v, 0.0) + jnp.log1p(jnp.exp(-jnp.abs(v)))
    decay = -jnp.exp(a_log_ref[...]) * dt
    span = decay.shape[0]
    lower = lax.broadcasted_iota(jnp.int32, (span, span), 0) >= lax.broadcasted_iota(
        jnp.int32, (span, span), 1
    )
    cum = jnp.dot(
        lower.astype(F32), decay, precision=lax.Precision.HIGHEST, preferred_element_type=F32
    )
    end = cum[span - 1 :, :]
    tok_ref[0] = cum
    tok_ref[1] = jnp.exp(end - cum) * dt
    tok_ref[2] = jnp.exp(cum)
    head_ref[0] = cum.T
    head_ref[1] = dt.T


def conv_tile(joined, rows, lanes, weight, bias):
    running = bias
    for tap in range(weight.shape[0]):
        start = EDGE - weight.shape[0] + 1 + tap
        running = running + weight[tap : tap + 1, :] * joined[pl.ds(start, rows), lanes]
    return silu(running)


def state_kernel(first_head, head_dim, groups, place, own_x, own_bc, *refs):
    shards = place.shape[0] - 1
    recv_refs = refs[: shards - 1]
    halo_x = refs[shards - 1 : 2 * shards - 1]
    halo_bc = refs[2 * shards - 1 : 3 * shards - 1]
    wx, bx, wbc, bbc, tok = refs[3 * shards - 1 : 3 * shards + 4]
    xc_ref, bcc_ref, own_ref, own_d_ref, send_ref = refs[3 * shards + 4 : 3 * shards + 9]
    joined, scaled, full, full_d = refs[3 * shards + 9 :]
    position, sub = place[0], place[1]
    rows, width = own_x.shape[1:]
    bc_width = own_bc.shape[2]
    span = SPAN
    edge = halo_x[0][...].astype(F32)
    edge_bc = halo_bc[0][...].astype(F32)
    for ref in halo_x[1:]:
        edge = edge + ref[...].astype(F32)
    for ref in halo_bc[1:]:
        edge_bc = edge_bc + ref[...].astype(F32)
    joined[:EDGE, :width] = edge
    joined[:EDGE, width:] = edge_bc
    at = pl.multiple_of(EDGE + position * rows, EDGE)
    joined[pl.ds(at, rows), :width] = own_x[0].astype(F32)
    joined[pl.ds(at, rows), width:] = own_bc[0].astype(F32)
    for k, ref in enumerate(recv_refs):
        source = lax.rem(position + shards - 1 - k, shards)
        at = pl.multiple_of(EDGE + source * rows, EDGE)
        joined[pl.ds(at, rows), :] = ref[...].astype(F32)
    for j in range(bc_width // LANES):
        lanes = slice(j * LANES, (j + 1) * LANES)
        inner = slice(width + j * LANES, width + (j + 1) * LANES)
        bcc_ref[:, lanes] = conv_tile(joined, span, inner, wbc[:, lanes], bbc[:, lanes]).astype(BF16)
    to_end = tok[1]
    last = tok[2, span - EDGE :, :]
    lane = lane_index(span)
    lane_few = lane_index(EDGE)
    for j in range(width // LANES):
        lanes = slice(j * LANES, (j + 1) * LANES)
        xc = conv_tile(joined, span, lanes, wx[:, lanes], bx[:, lanes]).astype(BF16)
        xc_ref[:, lanes] = xc
        head = first_head + j * (LANES // head_dim)
        factor = widen_pair(to_end, head, head_dim, lane)
        scaled[:, lanes] = (factor * xc.astype(F32)).astype(BF16)
        full_d[:, lanes] = widen_pair(last, head, head_dim, lane_few)
    group_width = width // groups
    for g in range(groups):
        b_in = bcc_ref[:, g * 2 * STATE : g * 2 * STATE + STATE].astype(F32)
        lanes = slice(g * group_width, (g + 1) * group_width)
        full[:, lanes] = jnp.dot(b_in.T.astype(BF16), scaled[:, lanes], preferred_element_type=F32)
    half = width // 2
    mine = pl.ds(pl.multiple_of(sub * half, LANES), half)
    other = pl.ds(pl.multiple_of((1 - sub) * half, LANES), half)
    own_ref[...] = full[:, mine]
    own_d_ref[...] = full_d[EDGE - 1 :, mine]
    send_ref[:STATE, :] = full[:, other].astype(BF16)
    d = full_d[EDGE - 1 :, other]
    high = d.astype(BF16)
    middle = (d - high.astype(F32)).astype(BF16)
    low = (d - high.astype(F32) - middle.astype(F32)).astype(BF16)
    row = lax.broadcasted_iota(jnp.int32, (EXTRA, half), 0)
    parts = jnp.where(row == 0, high.astype(F32), 0.0)
    parts = jnp.where(row == 1, middle.astype(F32), parts)
    parts = jnp.where(row == 2, low.astype(F32), parts)
    send_ref[STATE:, :] = parts.astype(BF16)


def intra_kernel(first_head, head_dim, groups, xc_ref, bcc_ref, tok, heads_ref, skip_ref, y_ref):
    span, width = xc_ref.shape
    per_strip = LANES // head_dim
    lane = lane_index(span)
    group_width = width // groups
    causal = lax.broadcasted_iota(jnp.int32, (span, span), 0) >= lax.broadcasted_iota(
        jnp.int32, (span, span), 1
    )
    cum = tok[0]
    for g in range(groups):
        b_in = bcc_ref[:, g * 2 * STATE : g * 2 * STATE + STATE]
        c_out = bcc_ref[:, g * 2 * STATE + STATE : (g + 1) * 2 * STATE]
        inner = lax.dot_general(
            c_out, b_in, (((1,), (1,)), ((), ())), preferred_element_type=F32
        )
        inner = jnp.where(causal, inner, 0.0)
        for j in range(g * group_width // LANES, (g + 1) * group_width // LANES):
            lanes = slice(j * LANES, (j + 1) * LANES)
            xc = xc_ref[:, lanes]
            wide = xc.astype(F32)
            mixes, rights = [], []
            for k in range(per_strip):
                head = first_head + j * per_strip + k
                gap = cum[:, head : head + 1] - heads_ref[0, head : head + 1, :]
                weight = jnp.exp(jnp.minimum(gap, 0.0)) * heads_ref[1, head : head + 1, :]
                mixes.append((inner * weight).astype(BF16))
                own = (lane >= k * head_dim) & (lane < (k + 1) * head_dim)
                rights.append(jnp.where(own, wide, 0.0).astype(BF16))
            y = jnp.dot(
                jnp.concatenate(mixes, axis=1),
                jnp.concatenate(rights, axis=0),
                preferred_element_type=F32,
            )
            head = first_head + j * per_strip
            skip = widen_pair(skip_ref[...], head, head_dim, lane_index(1))
            y_ref[:, lanes] = y + skip * wide


def finish_kernel(first_head, head_dim, groups, place, y_ref, bcc_ref, tok, mine, other, gain, *refs):
    out_ref, carried, scratch = refs[-3:]
    span, width = y_ref.shape
    half = width // 2
    sub = place[1]
    carried[:, pl.ds(pl.multiple_of(sub * half, LANES), half)] = mine[...]
    carried[:, pl.ds(pl.multiple_of((1 - sub) * half, LANES), half)] = other[...]
    lane = lane_index(span)
    group_width = width // groups
    decay = tok[2]
    for g in range(groups):
        c_out = bcc_ref[:, g * 2 * STATE + STATE : (g + 1) * 2 * STATE]
        lanes = slice(g * group_width, (g + 1) * group_width)
        scratch[...] = jnp.dot(c_out, carried[:, lanes], preferred_element_type=F32)
        squares = jnp.zeros((span, LANES), F32)
        for j in range(group_width // LANES):
            here = slice(j * LANES, (j + 1) * LANES)
            there = slice(g * group_width + j * LANES, g * group_width + (j + 1) * LANES)
            head = first_head + (g * group_width + j * LANES) // head_dim
            y = y_ref[:, there] + scratch[:, here] * widen_pair(decay, head, head_dim, lane)
            scratch[:, here] = y
            squares = squares + y * y
        mean = jnp.sum(squares, axis=1, keepdims=True) * (1.0 / group_width)
        factor = lax.rsqrt(mean + NORM_EPSILON)
        for j in range(group_width // LANES):
            here = slice(j * LANES, (j + 1) * LANES)
            there = slice(g * group_width + j * LANES, g * group_width + (j + 1) * LANES)
            out_ref[0, :, there] = (scratch[:, here] * factor * gain[:, there]).astype(BF16)


def on_device(
    x_raw,
    bc_raw,
    dt_raw,
    conv_x_weight,
    conv_x_bias,
    conv_bc_weight,
    conv_bc_bias,
    stride_offset_per_head,
    a_log,
    skip_d,
    norm_gain,
):
    shards = lax.axis_size("head")
    chips = lax.axis_size("seq")
    position = lax.axis_index("head")
    sub = lax.axis_index("sub")
    rows = x_raw.shape[1]
    width = conv_x_weight.shape[1]
    bc_width = conv_bc_weight.shape[1]
    heads = a_log.shape[0]
    head_dim = width // heads
    groups = bc_width // (2 * STATE)
    chunks = min(CHUNKS, groups)
    cw, cb, cg, ch = width // chunks, bc_width // chunks, groups // chunks, heads // chunks
    half = cw // 2
    taps = conv_x_weight.shape[0]
    place = jnp.stack([position, sub] + [position] * (shards - 1)).astype(jnp.int32)
    vmem = pl.BlockSpec(memory_space=pltpu.VMEM)
    row = lambda a: a.reshape(1, a.shape[0])

    def exchange(build):
        received = []
        for k in range(1, shards):
            target = lax.rem(position + k, shards)
            pairs = [(i, (i + k) % shards) for i in range(shards)]
            received.append(lax.ppermute(build(target), "head", pairs))
        return received

    dt_recv = exchange(lambda target: dt_raw[0])

    def payload(c):
        def build(target):
            x = lax.dynamic_slice(x_raw[0], (0, target * width + c * cw), (rows, cw))
            bc = lax.dynamic_slice(bc_raw[0], (0, target * bc_width + c * cb), (rows, cb))
            return jnp.concatenate([x, bc], axis=1)

        return build

    recvs = [exchange(payload(c)) for c in range(chunks)]

    pairs_of = lambda k: [
        ((b * shards + shards - 1) * 2 + s, ((b + s) * shards + k) * 2 + 1 - s)
        for b in range(chips)
        for s in range(2)
        if b + s < chips
    ]
    halos = []
    for k in range(shards):
        tail = jnp.concatenate(
            [
                x_raw[0, rows - EDGE :, k * width : (k + 1) * width],
                bc_raw[0, rows - EDGE :, k * bc_width : (k + 1) * bc_width],
            ],
            axis=1,
        )
        halos.append(lax.ppermute(tail, ("seq", "head", "sub"), pairs_of(k)))

    tok, by_head = pl.pallas_call(
        functools.partial(tables_kernel, heads),
        grid_spec=pltpu.PrefetchScalarGridSpec(
            num_scalar_prefetch=1,
            grid=(),
            in_specs=[vmem] * (shards + 2),
            out_specs=[vmem] * 2,
            scratch_shapes=[pltpu.VMEM((SPAN, dt_raw.shape[2]), F32)],
        ),
        out_shape=[
            jax.ShapeDtypeStruct((3, SPAN, heads), F32),
            jax.ShapeDtypeStruct((2, heads, SPAN), F32),
        ],
        name="tables",
    )(place, dt_raw, *dt_recv, row(stride_offset_per_head), row(a_log))

    wx, bx = conv_x_weight, row(conv_x_bias)
    wbc, bbc = conv_bc_weight, row(conv_bc_bias)

    def state(c):
        here = lambda i, place: (0, c)
        spec = lambda shape, index: pl.BlockSpec(shape, index)
        return pl.pallas_call(
            functools.partial(state_kernel, c * ch, head_dim, cg),
            grid_spec=pltpu.PrefetchScalarGridSpec(
                num_scalar_prefetch=1,
                grid=(1,),
                in_specs=[
                    spec((1, rows, cw), lambda i, place: (0, 0, place[0] * chunks + c)),
                    spec((1, rows, cb), lambda i, place: (0, 0, place[0] * chunks + c)),
                ]
                + [spec((rows, cw + cb), lambda i, place: (0, 0))] * (shards - 1)
                + [spec((EDGE, cw), here)] * shards
                + [spec((EDGE, cb), lambda i, place: (0, width // cb + c))] * shards
                + [
                    spec((taps, cw), here),
                    spec((1, cw), here),
                    spec((taps, cb), here),
                    spec((1, cb), here),
                    spec((3, SPAN, heads), lambda i, place: (0, 0, 0)),
                ],
                out_specs=[
                    spec((SPAN, cw), lambda i, place: (0, 0)),
                    spec((SPAN, cb), lambda i, place: (0, 0)),
                    spec((STATE, half), lambda i, place: (0, 0)),
                    spec((1, half), lambda i, place: (0, 0)),
                    spec((STATE + EXTRA, half), lambda i, place: (0, 0)),
                ],
                scratch_shapes=[
                    pltpu.VMEM((EDGE + SPAN, cw + cb), F32),
                    pltpu.VMEM((SPAN, cw), BF16),
                    pltpu.VMEM((STATE, cw), F32),
                    pltpu.VMEM((EDGE, cw), F32),
                ],
            ),
            out_shape=[
                jax.ShapeDtypeStruct((SPAN, cw), BF16),
                jax.ShapeDtypeStruct((SPAN, cb), BF16),
                jax.ShapeDtypeStruct((STATE, half), F32),
                jax.ShapeDtypeStruct((1, half), F32),
                jax.ShapeDtypeStruct((STATE + EXTRA, half), BF16),
            ],
            name=f"state_{c}",
        )(place, x_raw, bc_raw, *recvs[c], *halos, *halos, wx, bx, wbc, bbc, tok)

    even = sub == 0

    def swap(value):
        return lax.ppermute(value, "sub", [(0, 1), (1, 0)])

    def chain(own, own_d, send):
        got = swap(send)
        other = got[:STATE].astype(F32)
        other_d = jnp.sum(got[STATE : STATE + 3].astype(F32), axis=0, keepdims=True)
        state_even = jnp.where(even, own, other)
        state_odd = jnp.where(even, other, own)
        decay_even = jnp.where(even, own_d, other_d)
        decay_odd = jnp.where(even, other_d, own_d)
        total = decay_odd * state_even + state_odd
        decay = decay_even * decay_odd
        running = total
        entry = jnp.zeros((STATE, half), F32)
        for step in range(chips - 1):
            arrived = lax.ppermute(running.astype(BF16), "seq", [(step, step + 1)]).astype(F32)
            entry = entry + arrived
            running = decay * arrived + total
        later = decay_even * entry + state_even
        mine = jnp.where(even, entry, later).astype(BF16)
        theirs = swap(jnp.where(even, later, entry).astype(BF16))
        return mine, theirs

    def intra(c, xc, bcc):
        return pl.pallas_call(
            functools.partial(intra_kernel, c * ch, head_dim, cg),
            in_specs=[vmem] * 5,
            out_specs=vmem,
            out_shape=jax.ShapeDtypeStruct((SPAN, cw), F32),
            name=f"intra_{c}",
        )(xc, bcc, tok, by_head, row(skip_d))

    def finish(c, y, bcc, mine, theirs, out):
        full = lambda a: pl.BlockSpec(a.shape, lambda i, place: (0,) * a.ndim)
        before = [] if out is None else [out]
        return pl.pallas_call(
            functools.partial(finish_kernel, c * ch, head_dim, cg),
            grid_spec=pltpu.PrefetchScalarGridSpec(
                num_scalar_prefetch=1,
                grid=(1,),
                in_specs=[full(y), full(bcc), full(tok), full(mine), full(theirs)]
                + [pl.BlockSpec((1, cw), lambda i, place: (0, c))]
                + [pl.BlockSpec(memory_space=pl.ANY)] * len(before),
                out_specs=pl.BlockSpec((1, SPAN, cw), lambda i, place: (0, 0, c)),
                scratch_shapes=[
                    pltpu.VMEM((STATE, cw), BF16),
                    pltpu.VMEM((SPAN, cw // cg), F32),
                ],
            ),
            out_shape=jax.ShapeDtypeStruct((1, SPAN, width), BF16),
            input_output_aliases={7: 0} if before else {},
            name=f"finish_{c}",
        )(place, y, bcc, tok, mine, theirs, row(norm_gain), *before)

    parts = []
    for c in range(chunks):
        xc, bcc, own, own_d, send = state(c)
        mine, theirs = chain(own, own_d, send)
        parts.append((intra(c, xc, bcc), bcc, mine, theirs))
    out = None
    for c in range(chunks):
        out = finish(c, *parts[c], out)
    return out


def solution(mesh):
    placed = (
        P(("groups", "seq", "sub"), "head", None),
        P(("groups", "seq", "sub"), "head", None),
        P(("groups", "seq", "sub"), "head", None),
        P(None, "head"),
        P("head"),
        P(None, "head"),
        P("head"),
        P("head"),
        P("head"),
        P("head"),
        P("head"),
    )
    return jax.shard_map(
        on_device,
        mesh=mesh,
        in_specs=placed,
        out_specs=P(("groups", "seq", "sub"), None, "head"),
        check_vma=False,
    )
```

```python
import functools

import jax
import jax.numpy as jnp
from jax import lax
from jax.experimental import pallas as pl
from jax.experimental.pallas import tpu as pltpu
from jax.sharding import PartitionSpec as P


STATE = 128
SPAN = 128
LANES = 128
EDGE = 8
EXTRA = 16
NORM_EPSILON = 1e-05
CHUNKS = 2
VMEM_LIMIT = 8 * 1024 * 1024


F32 = jnp.float32
BF16 = jnp.bfloat16


def silu(v):
    return v / (1.0 + jnp.exp(-v))


def widen_pair(table, head, head_dim, lanes):
    count = LANES // head_dim
    strip = jnp.broadcast_to(table[:, head : head + 1], (table.shape[0], LANES))
    for k in range(1, count):
        column = jnp.broadcast_to(table[:, head + k : head + k + 1], (table.shape[0], LANES))
        strip = jnp.where(lanes >= k * head_dim, column, strip)
    return strip


def lane_index(rows):
    return lax.broadcasted_iota(jnp.int32, (rows, LANES), 1)


def tables_kernel(heads, place, own_ref, *refs):
    *recv_refs, offset_ref, a_log_ref, tok_ref, head_ref, raw = refs
    position = place[0]
    rows = own_ref.shape[1]
    shards = len(recv_refs) + 1
    raw[pl.ds(pl.multiple_of(position * rows, rows), rows), :] = own_ref[0].astype(F32)
    for k, ref in enumerate(recv_refs):
        source = lax.rem(position + shards - 1 - k, shards)
        raw[pl.ds(pl.multiple_of(source * rows, rows), rows), :] = ref[...].astype(F32)
    logits = raw[...]
    if shards > 1:
        total = logits.shape[1]
        logits = pltpu.roll(logits, lax.rem(total - position * heads, total), axis=1)
    v = logits[:, :heads] + offset_ref[...]
    dt = jnp.maximum(v, 0.0) + jnp.log1p(jnp.exp(-jnp.abs(v)))
    decay = -jnp.exp(a_log_ref[...]) * dt
    span = decay.shape[0]
    lower = lax.broadcasted_iota(jnp.int32, (span, span), 0) >= lax.broadcasted_iota(
        jnp.int32, (span, span), 1
    )
    cum = jnp.dot(
        lower.astype(F32), decay, precision=lax.Precision.HIGHEST, preferred_element_type=F32
    )
    end = cum[span - 1 :, :]
    tok_ref[0] = cum
    tok_ref[1] = jnp.exp(end - cum) * dt
    tok_ref[2] = jnp.exp(cum)
    head_ref[0] = cum.T
    head_ref[1] = dt.T


def conv_tile(joined, rows, lanes, weight, bias):
    running = bias
    for tap in range(weight.shape[0]):
        start = EDGE - weight.shape[0] + 1 + tap
        running = running + weight[tap : tap + 1, :] * joined[pl.ds(start, rows), lanes]
    return silu(running)


def state_kernel(c, head_dim, groups, place, own_x, own_bc, *refs):
    shards = place.shape[0] - 1
    recv_refs, halos = refs[: shards - 1], refs[shards - 1 : 2 * shards - 1]
    wx_ref, bx_ref, wbc_ref, bbc_ref, tok = refs[2 * shards - 1 : 2 * shards + 4]
    xc_ref, bcc_ref, own_ref, own_d_ref, send_ref = refs[2 * shards + 4 : 2 * shards + 9]
    joined, scaled, full, full_d = refs[2 * shards + 9 :]
    position, sub = place[0], place[1]
    rows = own_x.shape[1]
    width, bc_width = xc_ref.shape[1], bcc_ref.shape[1]
    all_width, all_bc = wx_ref.shape[1], wbc_ref.shape[1]
    first_head = c * width // head_dim
    columns, bc_columns = slice(c * width, (c + 1) * width), slice(c * bc_width, (c + 1) * bc_width)
    wx, bx = wx_ref[:, columns], bx_ref[:, columns]
    wbc, bbc = wbc_ref[:, bc_columns], bbc_ref[:, bc_columns]
    span = SPAN
    edge = halos[0][...].astype(F32)
    for ref in halos[1:]:
        edge = edge + ref[...].astype(F32)
    edge_bc = edge[:, all_width + c * bc_width : all_width + (c + 1) * bc_width]
    edge = edge[:, columns]
    own_columns = pl.ds(pl.multiple_of(position * all_width + c * width, LANES), width)
    own_bc_columns = pl.ds(pl.multiple_of(position * all_bc + c * bc_width, LANES), bc_width)
    joined[:EDGE, :width] = edge
    joined[:EDGE, width:] = edge_bc
    at = pl.multiple_of(EDGE + position * rows, EDGE)
    joined[pl.ds(at, rows), :width] = own_x[0, :, own_columns].astype(F32)
    joined[pl.ds(at, rows), width:] = own_bc[0, :, own_bc_columns].astype(F32)
    for k, ref in enumerate(recv_refs):
        source = lax.rem(position + shards - 1 - k, shards)
        at = pl.multiple_of(EDGE + source * rows, EDGE)
        joined[pl.ds(at, rows), :] = ref[...].astype(F32)
    for j in range(bc_width // LANES):
        lanes = slice(j * LANES, (j + 1) * LANES)
        inner = slice(width + j * LANES, width + (j + 1) * LANES)
        bcc_ref[:, lanes] = conv_tile(joined, span, inner, wbc[:, lanes], bbc[:, lanes]).astype(BF16)
    to_end = tok[1]
    last = tok[2, span - EDGE :, :]
    lane = lane_index(span)
    lane_few = lane_index(EDGE)
    for j in range(width // LANES):
        lanes = slice(j * LANES, (j + 1) * LANES)
        xc = conv_tile(joined, span, lanes, wx[:, lanes], bx[:, lanes]).astype(BF16)
        xc_ref[:, lanes] = xc
        head = first_head + j * (LANES // head_dim)
        factor = widen_pair(to_end, head, head_dim, lane)
        scaled[:, lanes] = (factor * xc.astype(F32)).astype(BF16)
        full_d[:, lanes] = widen_pair(last, head, head_dim, lane_few)
    group_width = width // groups
    for g in range(groups):
        b_in = bcc_ref[:, g * 2 * STATE : g * 2 * STATE + STATE].astype(F32)
        lanes = slice(g * group_width, (g + 1) * group_width)
        full[:, lanes] = jnp.dot(b_in.T.astype(BF16), scaled[:, lanes], preferred_element_type=F32)
    half = width // 2
    mine = pl.ds(pl.multiple_of(sub * half, LANES), half)
    other = pl.ds(pl.multiple_of((1 - sub) * half, LANES), half)
    own_ref[...] = full[:, mine]
    own_d_ref[...] = full_d[EDGE - 1 :, mine]
    send_ref[:STATE, :] = full[:, other].astype(BF16)
    d = full_d[EDGE - 1 :, other]
    high = d.astype(BF16)
    middle = (d - high.astype(F32)).astype(BF16)
    low = (d - high.astype(F32) - middle.astype(F32)).astype(BF16)
    row = lax.broadcasted_iota(jnp.int32, (EXTRA, half), 0)
    parts = jnp.where(row == 0, high.astype(F32), 0.0)
    parts = jnp.where(row == 1, middle.astype(F32), parts)
    parts = jnp.where(row == 2, low.astype(F32), parts)
    send_ref[STATE:, :] = parts.astype(BF16)


def intra_kernel(first_head, head_dim, groups, place, xc_ref, bcc_ref, tok, heads_ref, skip_ref, y_ref):
    span, width = xc_ref.shape
    per_strip = LANES // head_dim
    lane = lane_index(span)
    group_width = width // groups
    causal = lax.broadcasted_iota(jnp.int32, (span, span), 0) >= lax.broadcasted_iota(
        jnp.int32, (span, span), 1
    )
    cum = tok[0]
    for g in range(groups):
        b_in = bcc_ref[:, g * 2 * STATE : g * 2 * STATE + STATE]
        c_out = bcc_ref[:, g * 2 * STATE + STATE : (g + 1) * 2 * STATE]
        inner = lax.dot_general(
            c_out, b_in, (((1,), (1,)), ((), ())), preferred_element_type=F32
        )
        inner = jnp.where(causal, inner, 0.0)
        for j in range(g * group_width // LANES, (g + 1) * group_width // LANES):
            lanes = slice(j * LANES, (j + 1) * LANES)
            xc = xc_ref[:, lanes]
            wide = xc.astype(F32)
            mixes, rights = [], []
            for k in range(per_strip):
                head = first_head + j * per_strip + k
                gap = cum[:, head : head + 1] - heads_ref[0, head : head + 1, :]
                weight = jnp.exp(jnp.minimum(gap, 0.0)) * heads_ref[1, head : head + 1, :]
                mixes.append((inner * weight).astype(BF16))
                own = (lane >= k * head_dim) & (lane < (k + 1) * head_dim)
                rights.append(jnp.where(own, wide, 0.0).astype(BF16))
            y = jnp.dot(
                jnp.concatenate(mixes, axis=1),
                jnp.concatenate(rights, axis=0),
                preferred_element_type=F32,
            )
            head = first_head + j * per_strip
            skip = widen_pair(skip_ref[...], head, head_dim, lane_index(1))
            y_ref[:, lanes] = y + skip * wide


def finish_kernel(c, head_dim, groups, place, y_ref, bcc_ref, tok, mine, other, gain_ref, *refs):
    out_ref, carried, scratch, normed, sems = refs[-5:]
    span, width = y_ref.shape
    first_head = c * width // head_dim
    gain = gain_ref[:, c * width : (c + 1) * width]
    copies = []
    half = width // 2
    sub = place[1]
    carried[:, pl.ds(pl.multiple_of(sub * half, LANES), half)] = mine[...]
    carried[:, pl.ds(pl.multiple_of((1 - sub) * half, LANES), half)] = other[...]
    lane = lane_index(span)
    group_width = width // groups
    decay = tok[2]
    for g in range(groups):
        c_out = bcc_ref[:, g * 2 * STATE + STATE : (g + 1) * 2 * STATE]
        lanes = slice(g * group_width, (g + 1) * group_width)
        scratch[...] = jnp.dot(c_out, carried[:, lanes], preferred_element_type=F32)
        squares = jnp.zeros((span, LANES), F32)
        for j in range(group_width // LANES):
            here = slice(j * LANES, (j + 1) * LANES)
            there = slice(g * group_width + j * LANES, g * group_width + (j + 1) * LANES)
            head = first_head + (g * group_width + j * LANES) // head_dim
            y = y_ref[:, there] + scratch[:, here] * widen_pair(decay, head, head_dim, lane)
            scratch[:, here] = y
            squares = squares + y * y
        mean = jnp.sum(squares, axis=1, keepdims=True) * (1.0 / group_width)
        factor = lax.rsqrt(mean + NORM_EPSILON)
        for j in range(group_width // LANES):
            here = slice(j * LANES, (j + 1) * LANES)
            there = slice(g * group_width + j * LANES, g * group_width + (j + 1) * LANES)
            normed[:, there] = (scratch[:, here] * factor * gain[:, there]).astype(BF16)
        target = slice(c * width + g * group_width, c * width + (g + 1) * group_width)
        copies.append(
            pltpu.make_async_copy(normed.at[:, lanes], out_ref.at[0, :, target], sems.at[g])
        )
        copies[-1].start()
    for copy in copies:
        copy.wait()


def pack_kernel(parts, place, *refs):
    sources, out, sems = refs[: len(parts)], refs[-2], refs[-1]
    copies = []
    column = 0
    for n, (source, (stride, offset, count)) in enumerate(zip(sources, parts)):
        start = pl.multiple_of(place[0] * stride + offset, LANES)
        copies.append(
            pltpu.make_async_copy(
                source.at[0, :, pl.ds(start, count)], out.at[:, pl.ds(column, count)], sems.at[n]
            )
        )
        column += count
    for copy in copies:
        copy.start()
    for copy in copies:
        copy.wait()


def on_device(
    x_raw,
    bc_raw,
    dt_raw,
    conv_x_weight,
    conv_x_bias,
    conv_bc_weight,
    conv_bc_bias,
    stride_offset_per_head,
    a_log,
    skip_d,
    norm_gain,
):
    shards = lax.axis_size("head")
    chips = lax.axis_size("seq")
    position = lax.axis_index("head")
    sub = lax.axis_index("sub")
    rows = x_raw.shape[1]
    width = conv_x_weight.shape[1]
    bc_width = conv_bc_weight.shape[1]
    heads = a_log.shape[0]
    head_dim = width // heads
    groups = bc_width // (2 * STATE)
    chunks = min(CHUNKS, groups)
    cw, cb, cg, ch = width // chunks, bc_width // chunks, groups // chunks, heads // chunks
    half = cw // 2
    place = jnp.stack([position, sub] + [position] * (shards - 1)).astype(jnp.int32)
    row = lambda a: a.reshape(1, a.shape[0])
    even = sub == 0
    anywhere = pl.BlockSpec(memory_space=pl.ANY)
    vmem = pl.BlockSpec(memory_space=pltpu.VMEM)

    def call(kernel, operands, outs, scratch=(), specs=None, out_specs=None, aliases={}):
        return pl.pallas_call(
            kernel,
            grid_spec=pltpu.PrefetchScalarGridSpec(
                num_scalar_prefetch=1,
                grid=(),
                in_specs=specs or [vmem] * (len(operands) - 1),
                out_specs=out_specs or [vmem] * len(outs),
                scratch_shapes=list(scratch),
            ),
            out_shape=list(outs),
            input_output_aliases=aliases,
            compiler_params=pltpu.CompilerParams(vmem_limit_bytes=VMEM_LIMIT),
        )(*operands)

    def shift(k):
        return [(i, (i + k) % shards) for i in range(shards)]

    def send_chunk(c):
        received = []
        for k in range(1, shards):
            target = lax.rem(position + k, shards).astype(jnp.int32).reshape(1)
            (packed,) = call(
                functools.partial(pack_kernel, ((width, c * cw, cw), (bc_width, c * cb, cb))),
                (target, x_raw, bc_raw),
                [pltpu.VMEM((rows, cw + cb), BF16)],
                [pltpu.SemaphoreType.DMA((2,))],
                specs=[pl.BlockSpec(memory_space=pltpu.HBM)] * 2,
            )
            received.append(lax.ppermute(packed, "head", shift(k)))
        return received

    recvs = [send_chunk(c) for c in range(chunks)]
    dt_recv = [lax.ppermute(dt_raw[0], "head", shift(k)) for k in range(1, shards)]

    following = lambda k: [
        ((b * shards + shards - 1) * 2 + s, ((b + s) * shards + k) * 2 + 1 - s)
        for b in range(chips)
        for s in range(2)
        if b + s < chips
    ]
    halos = []
    for k in range(shards):
        tail = jnp.concatenate(
            [
                x_raw[0, rows - EDGE :, k * width : (k + 1) * width],
                bc_raw[0, rows - EDGE :, k * bc_width : (k + 1) * bc_width],
            ],
            axis=1,
        )
        halos.append(lax.ppermute(tail, ("seq", "head", "sub"), following(k)))

    tok, by_head = call(
        functools.partial(tables_kernel, heads),
        (place, dt_raw, *dt_recv, row(stride_offset_per_head), row(a_log)),
        [pltpu.VMEM((3, SPAN, heads), F32), pltpu.VMEM((2, heads, SPAN), F32)],
        [pltpu.VMEM((SPAN, dt_raw.shape[2]), F32)],
    )

    weights = (conv_x_weight, row(conv_x_bias), conv_bc_weight, row(conv_bc_bias))

    def state(c):
        return call(
            functools.partial(state_kernel, c, head_dim, cg),
            (place, x_raw, bc_raw, *recvs[c], *halos, *weights, tok),
            [
                pltpu.VMEM((SPAN, cw), BF16),
                pltpu.VMEM((SPAN, cb), BF16),
                pltpu.VMEM((STATE, half), F32),
                pltpu.VMEM((1, half), F32),
                pltpu.VMEM((STATE + EXTRA, half), BF16),
            ],
            [
                pltpu.VMEM((EDGE + SPAN, cw + cb), F32),
                pltpu.VMEM((SPAN, cw), BF16),
                pltpu.VMEM((STATE, cw), F32),
                pltpu.VMEM((EDGE, cw), F32),
            ],
        )

    def chain(own, own_d, send):
        got = lax.ppermute(send, "sub", [(0, 1), (1, 0)])
        other = got[:STATE].astype(F32)
        other_d = jnp.sum(got[STATE : STATE + 3].astype(F32), axis=0, keepdims=True)
        state_even = jnp.where(even, own, other)
        state_odd = jnp.where(even, other, own)
        decay_even = jnp.where(even, own_d, other_d)
        decay_odd = jnp.where(even, other_d, own_d)
        total = decay_odd * state_even + state_odd
        decay = decay_even * decay_odd
        running = total
        entry = jnp.zeros((STATE, half), F32)
        for step in range(chips - 1):
            arrived = lax.ppermute(running.astype(BF16), "seq", [(step, step + 1)])
            arrived = arrived.astype(F32)
            entry = entry + arrived
            running = decay * arrived + total
        later = decay_even * entry + state_even
        mine = jnp.where(even, entry, later).astype(BF16)
        theirs = jnp.where(even, later, entry).astype(BF16)
        return mine, lax.ppermute(theirs, "sub", [(0, 1), (1, 0)])

    def intra(c, xc, bcc):
        return call(
            functools.partial(intra_kernel, c * ch, head_dim, cg),
            (place, xc, bcc, tok, by_head, row(skip_d)),
            [pltpu.VMEM((SPAN, cw), F32)],
        )[0]

    def finish(c, y, bcc, mine, theirs, out):
        before = [] if out is None else [out]
        return call(
            functools.partial(finish_kernel, c, head_dim, cg),
            (place, y, bcc, tok, mine, theirs, row(norm_gain), *before),
            [jax.ShapeDtypeStruct((1, SPAN, width), BF16)],
            [
                pltpu.VMEM((STATE, cw), BF16),
                pltpu.VMEM((SPAN, cw // cg), F32),
                pltpu.VMEM((SPAN, cw), BF16),
                pltpu.SemaphoreType.DMA((cg,)),
            ],
            specs=[vmem] * 6 + [anywhere] * len(before),
            out_specs=[anywhere],
            aliases={7: 0} if before else {},
        )[0]

    parts = []
    for c in range(chunks):
        xc, bcc, own, own_d, send = state(c)
        mine, theirs = chain(own, own_d, send)
        parts.append((intra(c, xc, bcc), bcc, mine, theirs))
    out = None
    for c in range(chunks):
        out = finish(c, *parts[c], out)
    return out


def solution(mesh):
    placed = (
        P(("groups", "seq", "sub"), "head", None),
        P(("groups", "seq", "sub"), "head", None),
        P(("groups", "seq", "sub"), "head", None),
        P(None, "head"),
        P("head"),
        P(None, "head"),
        P("head"),
        P("head"),
        P("head"),
        P("head"),
        P("head"),
    )
    return jax.shard_map(
        on_device,
        mesh=mesh,
        in_specs=placed,
        out_specs=P(("groups", "seq", "sub"), None, "head"),
        check_vma=False,
    )
```

```python
import functools

import jax
import jax.numpy as jnp
from jax import lax
from jax.experimental import pallas as pl
from jax.experimental.pallas import tpu as pltpu
from jax.sharding import PartitionSpec as P


STATE = 128
SPAN = 128
LANES = 128
EDGE = 8
EXTRA = 16
NORM_EPSILON = 1e-05
CHUNKS = 2
VMEM_LIMIT = 8 * 1024 * 1024


F32 = jnp.float32
BF16 = jnp.bfloat16


def silu(v):
    return v / (1.0 + jnp.exp(-v))


def widen_pair(table, head, head_dim, lanes):
    count = LANES // head_dim
    strip = jnp.broadcast_to(table[:, head : head + 1], (table.shape[0], LANES))
    for k in range(1, count):
        column = jnp.broadcast_to(table[:, head + k : head + k + 1], (table.shape[0], LANES))
        strip = jnp.where(lanes >= k * head_dim, column, strip)
    return strip


def lane_index(rows):
    return lax.broadcasted_iota(jnp.int32, (rows, LANES), 1)


def tables_kernel(heads, own_ref, *refs):
    *recv_refs, by_head, tok_ref, head_ref, raw = refs
    position = lax.axis_index("head")
    rows = own_ref.shape[1]
    shards = len(recv_refs) + 1
    raw[pl.ds(pl.multiple_of(position * rows, rows), rows), :] = own_ref[0].astype(F32)
    for k, ref in enumerate(recv_refs):
        source = lax.rem(position + shards - 1 - k, shards)
        raw[pl.ds(pl.multiple_of(source * rows, rows), rows), :] = ref[...].astype(F32)
    logits = raw[...]
    if shards > 1:
        total = logits.shape[1]
        logits = pltpu.roll(logits, lax.rem(total - position * heads, total), axis=1)
    v = logits[:, :heads] + by_head[0:1, :]
    dt = jnp.maximum(v, 0.0) + jnp.log1p(jnp.exp(-jnp.abs(v)))
    decay = -jnp.exp(by_head[1:2, :]) * dt
    span = decay.shape[0]
    lower = lax.broadcasted_iota(jnp.int32, (span, span), 0) >= lax.broadcasted_iota(
        jnp.int32, (span, span), 1
    )
    cum = jnp.dot(
        lower.astype(F32), decay, precision=lax.Precision.HIGHEST, preferred_element_type=F32
    )
    end = cum[span - 1 :, :]
    tok_ref[0] = cum
    tok_ref[1] = jnp.exp(end - cum) * dt
    tok_ref[2] = jnp.exp(cum)
    head_ref[0] = cum.T
    head_ref[1] = dt.T


def conv_tile(joined, rows, lanes, weight, bias):
    running = bias
    for tap in range(weight.shape[0]):
        start = EDGE - weight.shape[0] + 1 + tap
        running = running + weight[tap : tap + 1, :] * joined[pl.ds(start, rows), lanes]
    return silu(running)


def state_kernel(c, taps, all_width, head_dim, groups, shards, own_columns, *refs):
    recv_refs, halos = refs[: shards - 1], refs[shards - 1 : 2 * shards - 1]
    rows_ref, tok = refs[2 * shards - 1 : 2 * shards + 1]
    xc_ref, bcc_ref, own_ref, own_d_ref, send_ref = refs[2 * shards + 1 : 2 * shards + 6]
    joined, scaled, full, full_d = refs[2 * shards + 6 :]
    position, sub = lax.axis_index("head"), lax.axis_index("sub")
    rows = own_columns.shape[0]
    width, bc_width = xc_ref.shape[1], bcc_ref.shape[1]
    first_head = c * width // head_dim
    columns = slice(c * width, (c + 1) * width)
    bc_columns = slice(all_width + c * bc_width, all_width + (c + 1) * bc_width)
    wx, bx = rows_ref[:taps, columns], rows_ref[taps : taps + 1, columns]
    wbc, bbc = rows_ref[:taps, bc_columns], rows_ref[taps : taps + 1, bc_columns]
    span = SPAN
    edge = halos[0][:, columns].astype(F32)
    edge_bc = halos[0][:, bc_columns].astype(F32)
    for ref in halos[1:]:
        edge = edge + ref[:, columns].astype(F32)
        edge_bc = edge_bc + ref[:, bc_columns].astype(F32)
    joined[:EDGE, :width] = edge
    joined[:EDGE, width:] = edge_bc
    at = pl.multiple_of(EDGE + position * rows, EDGE)
    joined[pl.ds(at, rows), :width] = own_columns[:, columns].astype(F32)
    joined[pl.ds(at, rows), width:] = own_columns[:, bc_columns].astype(F32)
    for k, ref in enumerate(recv_refs):
        source = lax.rem(position + shards - 1 - k, shards)
        at = pl.multiple_of(EDGE + source * rows, EDGE)
        joined[pl.ds(at, rows), :] = ref[...].astype(F32)
    for j in range(bc_width // LANES):
        lanes = slice(j * LANES, (j + 1) * LANES)
        inner = slice(width + j * LANES, width + (j + 1) * LANES)
        bcc_ref[:, lanes] = conv_tile(joined, span, inner, wbc[:, lanes], bbc[:, lanes]).astype(BF16)
    to_end = tok[1]
    last = tok[2, span - EDGE :, :]
    lane = lane_index(span)
    lane_few = lane_index(EDGE)
    for j in range(width // LANES):
        lanes = slice(j * LANES, (j + 1) * LANES)
        xc = conv_tile(joined, span, lanes, wx[:, lanes], bx[:, lanes]).astype(BF16)
        xc_ref[:, lanes] = xc
        head = first_head + j * (LANES // head_dim)
        factor = widen_pair(to_end, head, head_dim, lane)
        scaled[:, lanes] = (factor * xc.astype(F32)).astype(BF16)
        full_d[:, lanes] = widen_pair(last, head, head_dim, lane_few)
    group_width = width // groups
    for g in range(groups):
        b_in = bcc_ref[:, g * 2 * STATE : g * 2 * STATE + STATE].astype(F32)
        lanes = slice(g * group_width, (g + 1) * group_width)
        full[:, lanes] = jnp.dot(b_in.T.astype(BF16), scaled[:, lanes], preferred_element_type=F32)
    half = width // 2
    mine = pl.ds(pl.multiple_of(sub * half, LANES), half)
    other = pl.ds(pl.multiple_of((1 - sub) * half, LANES), half)
    own_ref[...] = full[:, mine].astype(BF16)
    own_d_ref[...] = full_d[EDGE - 1 :, mine]
    send_ref[:STATE, :] = full[:, other].astype(BF16)
    d = full_d[EDGE - 1 :, other]
    high = d.astype(BF16)
    middle = (d - high.astype(F32)).astype(BF16)
    low = (d - high.astype(F32) - middle.astype(F32)).astype(BF16)
    row = lax.broadcasted_iota(jnp.int32, (EXTRA, half), 0)
    parts = jnp.where(row == 0, high.astype(F32), 0.0)
    parts = jnp.where(row == 1, middle.astype(F32), parts)
    parts = jnp.where(row == 2, low.astype(F32), parts)
    send_ref[STATE:, :] = parts.astype(BF16)


def intra_kernel(first_head, head_dim, groups, xc_ref, bcc_ref, tok, heads_ref, by_head, y_ref):
    span, width = xc_ref.shape
    per_strip = LANES // head_dim
    lane = lane_index(span)
    group_width = width // groups
    causal = lax.broadcasted_iota(jnp.int32, (span, span), 0) >= lax.broadcasted_iota(
        jnp.int32, (span, span), 1
    )
    cum = tok[0]
    for g in range(groups):
        b_in = bcc_ref[:, g * 2 * STATE : g * 2 * STATE + STATE]
        c_out = bcc_ref[:, g * 2 * STATE + STATE : (g + 1) * 2 * STATE]
        inner = lax.dot_general(
            c_out, b_in, (((1,), (1,)), ((), ())), preferred_element_type=F32
        )
        inner = jnp.where(causal, inner, 0.0)
        for j in range(g * group_width // LANES, (g + 1) * group_width // LANES):
            lanes = slice(j * LANES, (j + 1) * LANES)
            xc = xc_ref[:, lanes]
            wide = xc.astype(F32)
            mixes, rights = [], []
            for k in range(per_strip):
                head = first_head + j * per_strip + k
                gap = cum[:, head : head + 1] - heads_ref[0, head : head + 1, :]
                weight = jnp.exp(jnp.minimum(gap, 0.0)) * heads_ref[1, head : head + 1, :]
                mixes.append((inner * weight).astype(BF16))
                own = (lane >= k * head_dim) & (lane < (k + 1) * head_dim)
                rights.append(jnp.where(own, wide, 0.0).astype(BF16))
            y = jnp.dot(
                jnp.concatenate(mixes, axis=1),
                jnp.concatenate(rights, axis=0),
                preferred_element_type=F32,
            )
            head = first_head + j * per_strip
            skip = widen_pair(by_head[2:3, :], head, head_dim, lane_index(1))
            y_ref[:, lanes] = (y + skip * wide).astype(y_ref.dtype)


def finish_kernel(c, gain_row, head_dim, groups, y_ref, bcc_ref, tok, mine, other, rows_ref, *refs):
    out_ref, carried, scratch, normed, sems = refs[-5:]
    span, width = y_ref.shape
    first_head = c * width // head_dim
    gain = rows_ref[gain_row : gain_row + 1, c * width : (c + 1) * width]
    copies = []
    half = width // 2
    sub = lax.axis_index("sub")
    carried[:, pl.ds(pl.multiple_of(sub * half, LANES), half)] = mine[...]
    carried[:, pl.ds(pl.multiple_of((1 - sub) * half, LANES), half)] = other[...]
    lane = lane_index(span)
    group_width = width // groups
    decay = tok[2]
    for g in range(groups):
        c_out = bcc_ref[:, g * 2 * STATE + STATE : (g + 1) * 2 * STATE]
        lanes = slice(g * group_width, (g + 1) * group_width)
        scratch[...] = jnp.dot(c_out, carried[:, lanes], preferred_element_type=F32)
        squares = jnp.zeros((span, LANES), F32)
        for j in range(group_width // LANES):
            here = slice(j * LANES, (j + 1) * LANES)
            there = slice(g * group_width + j * LANES, g * group_width + (j + 1) * LANES)
            head = first_head + (g * group_width + j * LANES) // head_dim
            y = y_ref[:, there].astype(F32) + scratch[:, here] * widen_pair(decay, head, head_dim, lane)
            scratch[:, here] = y
            squares = squares + y * y
        mean = jnp.sum(squares, axis=1, keepdims=True) * (1.0 / group_width)
        factor = lax.rsqrt(mean + NORM_EPSILON)
        for j in range(group_width // LANES):
            here = slice(j * LANES, (j + 1) * LANES)
            there = slice(g * group_width + j * LANES, g * group_width + (j + 1) * LANES)
            normed[:, there] = (scratch[:, here] * factor * gain[:, there]).astype(BF16)
        target = slice(c * width + g * group_width, c * width + (g + 1) * group_width)
        copies.append(
            pltpu.make_async_copy(normed.at[:, lanes], out_ref.at[0, :, target], sems.at[g])
        )
        copies[-1].start()
    for copy in copies:
        copy.wait()


def copy_all(pairs, sems):
    copies = [pltpu.make_async_copy(a, b, sems.at[n]) for n, (a, b) in enumerate(pairs)]
    for copy in copies:
        copy.start()
    for copy in copies:
        copy.wait()


def pack_kernel(k, shards, parts, *refs):
    sources, out, sems = refs[: len(parts)], refs[-2], refs[-1]
    target = lax.rem(lax.axis_index("head") + k, shards)
    pairs = []
    column = 0
    for source, (stride, offset, count) in zip(sources, parts):
        start = pl.multiple_of(target * stride + offset, LANES)
        pairs.append((source.at[0, :, pl.ds(start, count)], out.at[:, pl.ds(column, count)]))
        column += count
    copy_all(pairs, sems)


def tails_kernel(width, bc_width, x_ref, bc_ref, *refs):
    *outs, sems = refs
    last = pl.ds(x_ref.shape[1] - EDGE, EDGE)
    pairs = []
    for k, out in enumerate(outs):
        pairs.append(
            (x_ref.at[0, last, pl.ds(k * width, width)], out.at[:, pl.ds(0, width)])
        )
        pairs.append(
            (bc_ref.at[0, last, pl.ds(k * bc_width, bc_width)], out.at[:, pl.ds(width, bc_width)])
        )
    copy_all(pairs, sems)


def partner_decay(got):
    rows = got[STATE:, :].astype(F32)
    return rows[0:1, :] + rows[1:2, :] + rows[2:3, :]


def join_kernel(own, own_d, got, total, decay):
    sub = lax.axis_index("sub")
    other_d = partner_decay(got)
    decay[...] = own_d[...] * other_d

    @pl.when(sub == 0)
    def _():
        total[...] = (other_d * own[...].astype(F32) + got[:STATE, :].astype(F32)).astype(BF16)

    @pl.when(sub != 0)
    def _():
        total[...] = (own_d[...] * got[:STATE, :].astype(F32) + own[...].astype(F32)).astype(BF16)


def relay_kernel(arrived, total, decay, out):
    out[...] = (decay[...] * arrived[...].astype(F32) + total[...].astype(F32)).astype(BF16)


def close_kernel(own, own_d, got, *refs):
    *arrived, mine, theirs, entry = refs
    chip, sub = lax.axis_index("seq"), lax.axis_index("sub")

    @pl.when(chip == 0)
    def _():
        entry[...] = jnp.zeros_like(entry)

    for step, ref in enumerate(arrived):

        @pl.when(chip == step + 1)
        def _():
            entry[...] = ref[...]

    @pl.when(sub == 0)
    def _():
        mine[...] = entry[...]
        theirs[...] = (own_d[...] * entry[...].astype(F32) + own[...].astype(F32)).astype(BF16)

    @pl.when(sub != 0)
    def _():
        theirs[...] = entry[...]
        mine[...] = (
            partner_decay(got) * entry[...].astype(F32) + got[:STATE, :].astype(F32)
        ).astype(BF16)


def prep_kernel(x_ref, bc_ref, wx, bx, wbc, bbc, gain, offset, a_log, skip, *refs):
    own_ref, rows_ref, heads_ref, sems = refs
    taps, width = wx.shape
    bc_width = wbc.shape[1]
    position = lax.axis_index("head")
    x_at = pl.multiple_of(position * width, LANES)
    bc_at = pl.multiple_of(position * bc_width, LANES)
    copies = [
        pltpu.make_async_copy(
            x_ref.at[0, :, pl.ds(x_at, width)], own_ref.at[:, pl.ds(0, width)], sems.at[0]
        ),
        pltpu.make_async_copy(
            bc_ref.at[0, :, pl.ds(bc_at, bc_width)], own_ref.at[:, pl.ds(width, bc_width)], sems.at[1]
        ),
    ]
    for copy in copies:
        copy.start()
    rows_ref[:taps, :width] = wx[...]
    rows_ref[taps : taps + 1, :width] = bx[...]
    rows_ref[taps + 1 : taps + 2, :width] = gain[...]
    rows_ref[:taps, width:] = wbc[...]
    rows_ref[taps : taps + 1, width:] = bbc[...]
    heads_ref[0:1, :] = offset[...]
    heads_ref[1:2, :] = a_log[...]
    heads_ref[2:3, :] = skip[...]
    for copy in copies:
        copy.wait()


def on_device(
    x_raw,
    bc_raw,
    dt_raw,
    conv_x_weight,
    conv_x_bias,
    conv_bc_weight,
    conv_bc_bias,
    stride_offset_per_head,
    a_log,
    skip_d,
    norm_gain,
):
    shards = lax.axis_size("head")
    chips = lax.axis_size("seq")
    rows = x_raw.shape[1]
    width = conv_x_weight.shape[1]
    bc_width = conv_bc_weight.shape[1]
    heads = a_log.shape[0]
    head_dim = width // heads
    groups = bc_width // (2 * STATE)
    chunks = min(CHUNKS, groups)
    cw, cb, cg, ch = width // chunks, bc_width // chunks, groups // chunks, heads // chunks
    half = cw // 2
    row = lambda a: a.reshape(1, a.shape[0])
    hbm = pl.BlockSpec(memory_space=pltpu.HBM)
    anywhere = pl.BlockSpec(memory_space=pl.ANY)
    vmem = pl.BlockSpec(memory_space=pltpu.VMEM)

    def call(kernel, operands, outs, scratch=(), specs=None, out_specs=None, aliases={}):
        return pl.pallas_call(
            kernel,
            in_specs=specs or [vmem] * len(operands),
            out_specs=out_specs or [vmem] * len(outs),
            scratch_shapes=list(scratch),
            out_shape=list(outs),
            input_output_aliases=aliases,
            compiler_params=pltpu.CompilerParams(vmem_limit_bytes=VMEM_LIMIT),
        )(*operands)

    def shift(k):
        return [(i, (i + k) % shards) for i in range(shards)]

    x_here = pltpu.with_memory_space_constraint(x_raw, pltpu.HBM)
    bc_here = pltpu.with_memory_space_constraint(bc_raw, pltpu.HBM)

    def send_chunk(c):
        received = []
        for k in range(1, shards):
            (packed,) = call(
                functools.partial(
                    pack_kernel, k, shards, ((width, c * cw, cw), (bc_width, c * cb, cb))
                ),
                (x_here, bc_here),
                [pltpu.VMEM((rows, cw + cb), BF16)],
                [pltpu.SemaphoreType.DMA((2,))],
                specs=[hbm] * 2,
            )
            received.append(lax.ppermute(packed, "head", shift(k)))
        return received

    dt_recv = [lax.ppermute(dt_raw[0], "head", shift(k)) for k in range(1, shards)]
    recvs = [send_chunk(c) for c in range(chunks)]
    taps = conv_x_weight.shape[0]
    own_columns, rows_table, heads_table = call(
        prep_kernel,
        (
            x_here,
            bc_here,
            conv_x_weight,
            row(conv_x_bias),
            conv_bc_weight,
            row(conv_bc_bias),
            row(norm_gain),
            row(stride_offset_per_head),
            row(a_log),
            row(skip_d),
        ),
        [
            pltpu.VMEM((rows, width + bc_width), BF16),
            pltpu.VMEM((8, width + bc_width), F32),
            pltpu.VMEM((8, heads), F32),
        ],
        [pltpu.SemaphoreType.DMA((2,))],
        specs=[hbm] * 2 + [vmem] * 8,
    )

    following = lambda k: [
        ((b * shards + shards - 1) * 2 + s, ((b + s) * shards + k) * 2 + 1 - s)
        for b in range(chips)
        for s in range(2)
        if b + s < chips
    ]
    tails = call(
        functools.partial(tails_kernel, width, bc_width),
        (x_here, bc_here),
        [pltpu.VMEM((EDGE, width + bc_width), BF16)] * shards,
        [pltpu.SemaphoreType.DMA((2 * shards,))],
        specs=[hbm] * 2,
    )
    halos = [lax.ppermute(tails[k], ("seq", "head", "sub"), following(k)) for k in range(shards)]

    tok, by_head = call(
        functools.partial(tables_kernel, heads),
        (dt_raw, *dt_recv, heads_table),
        [pltpu.VMEM((3, SPAN, heads), F32), pltpu.VMEM((2, heads, SPAN), F32)],
        [pltpu.VMEM((SPAN, dt_raw.shape[2]), F32)],
    )

    def state(c):
        return call(
            functools.partial(state_kernel, c, taps, width, head_dim, cg, shards),
            (own_columns, *recvs[c], *halos, rows_table, tok),
            [
                pltpu.VMEM((SPAN, cw), BF16),
                pltpu.VMEM((SPAN, cb), BF16),
                pltpu.VMEM((STATE, half), BF16),
                pltpu.VMEM((1, half), F32),
                pltpu.VMEM((STATE + EXTRA, half), BF16),
            ],
            [
                pltpu.VMEM((EDGE + SPAN, cw + cb), F32),
                pltpu.VMEM((SPAN, cw), BF16),
                pltpu.VMEM((STATE, cw), F32),
                pltpu.VMEM((EDGE, cw), F32),
            ],
        )

    def chain(own, own_d, send):
        got = lax.ppermute(send, "sub", [(0, 1), (1, 0)])
        state_shape = pltpu.VMEM((STATE, half), BF16)
        total, decay = call(
            join_kernel, (own, own_d, got), [state_shape, pltpu.VMEM((1, half), F32)]
        )
        running = total
        arrived = []
        for step in range(chips - 1):
            pairs = [(step, step + 1)]
            if step == 0 and chips % 2 == 0:
                pairs = [(i, i ^ 1) for i in range(chips)]
            arrived.append(lax.ppermute(running, "seq", pairs))
            if step < chips - 2:
                (running,) = call(relay_kernel, (arrived[-1], total, decay), [state_shape])
        mine, theirs = call(
            close_kernel,
            (own, own_d, got, *arrived),
            [state_shape] * 2,
            [pltpu.VMEM((STATE, half), BF16)],
        )
        return mine, lax.ppermute(theirs, "sub", [(0, 1), (1, 0)])

    def intra(c, xc, bcc):
        return call(
            functools.partial(intra_kernel, c * ch, head_dim, cg),
            (xc, bcc, tok, by_head, heads_table),
            [pltpu.VMEM((SPAN, cw), BF16)],
        )[0]

    def finish(c, y, bcc, mine, theirs, out):
        before = [] if out is None else [out]
        return call(
            functools.partial(finish_kernel, c, taps + 1, head_dim, cg),
            (y, bcc, tok, mine, theirs, rows_table, *before),
            [jax.ShapeDtypeStruct((1, SPAN, width), BF16)],
            [
                pltpu.VMEM((STATE, cw), BF16),
                pltpu.VMEM((SPAN, cw // cg), F32),
                pltpu.VMEM((SPAN, cw), BF16),
                pltpu.SemaphoreType.DMA((cg,)),
            ],
            specs=[vmem] * 6 + [anywhere] * len(before),
            out_specs=[anywhere],
            aliases={6: 0} if before else {},
        )[0]

    parts = []
    for c in range(chunks):
        xc, bcc, own, own_d, send = state(c)
        mine, theirs = chain(own, own_d, send)
        parts.append((intra(c, xc, bcc), bcc, mine, theirs))
    out = None
    for c in range(chunks):
        out = finish(c, *parts[c], out)
    return out


def solution(mesh):
    placed = (
        P(("groups", "seq", "sub"), "head", None),
        P(("groups", "seq", "sub"), "head", None),
        P(("groups", "seq", "sub"), "head", None),
        P(None, "head"),
        P("head"),
        P(None, "head"),
        P("head"),
        P("head"),
        P("head"),
        P("head"),
        P("head"),
    )
    return jax.shard_map(
        on_device,
        mesh=mesh,
        in_specs=placed,
        out_specs=P(("groups", "seq", "sub"), None, "head"),
        check_vma=False,
    )
```

```python
import functools

import jax
import jax.numpy as jnp
from jax import lax
from jax.experimental import pallas as pl
from jax.experimental.pallas import tpu as pltpu
from jax.sharding import PartitionSpec as P


STATE = 128
SPAN = 128
LANES = 128
EDGE = 8
EXTRA = 8
NORM_EPSILON = 1e-05
PIECES = 2
VMEM_LIMIT = 8 * 1024 * 1024


F32 = jnp.float32
BF16 = jnp.bfloat16


def plan_of(groups):
    return (groups - groups // 2, groups // 2) if groups > 1 else (groups,)


def silu(v):
    return v / (1.0 + jnp.exp(-v))


def widen_pair(table, head, head_dim, lanes):
    count = LANES // head_dim
    strip = jnp.broadcast_to(table[:, head : head + 1], (table.shape[0], LANES))
    for k in range(1, count):
        column = jnp.broadcast_to(table[:, head + k : head + k + 1], (table.shape[0], LANES))
        strip = jnp.where(lanes >= k * head_dim, column, strip)
    return strip


def lane_index(rows):
    return lax.broadcasted_iota(jnp.int32, (rows, LANES), 1)


def tables_kernel(heads, own_ref, *refs):
    *recv_refs, by_head, tok_ref, head_ref, raw = refs
    position = lax.axis_index("head")
    rows = own_ref.shape[1]
    shards = len(recv_refs) + 1
    raw[pl.ds(pl.multiple_of(position * rows, rows), rows), :] = own_ref[0].astype(F32)
    for k, ref in enumerate(recv_refs):
        source = lax.rem(position + shards - 1 - k, shards)
        raw[pl.ds(pl.multiple_of(source * rows, rows), rows), :] = ref[...].astype(F32)
    logits = raw[...]
    if shards > 1:
        total = logits.shape[1]
        logits = pltpu.roll(logits, lax.rem(total - position * heads, total), axis=1)
    v = logits[:, :heads] + by_head[0:1, :]
    dt = jnp.maximum(v, 0.0) + jnp.log1p(jnp.exp(-jnp.abs(v)))
    decay = -jnp.exp(by_head[1:2, :]) * dt
    span = decay.shape[0]
    lower = lax.broadcasted_iota(jnp.int32, (span, span), 0) >= lax.broadcasted_iota(
        jnp.int32, (span, span), 1
    )
    cum = jnp.dot(
        lower.astype(F32), decay, precision=lax.Precision.HIGHEST, preferred_element_type=F32
    )
    end = cum[span - 1 :, :]
    tok_ref[0] = cum
    tok_ref[1] = jnp.exp(end - cum) * dt
    tok_ref[2] = jnp.exp(cum)
    head_ref[0] = cum.T
    head_ref[1] = dt.T


def conv_tile(joined, rows, lanes, weight, bias):
    running = bias
    for tap in range(weight.shape[0]):
        start = EDGE - weight.shape[0] + 1 + tap
        running = running + weight[tap : tap + 1, :] * joined[pl.ds(start, rows), lanes]
    return silu(running)


def state_kernel(which, first, taps, all_width, head_dim, groups, shards, own_columns, *refs):
    chip = lax.axis_index("seq")
    body = functools.partial(
        block_state, first, taps, all_width, head_dim, groups, shards, own_columns
    )
    if which == "first":
        pl.when(chip == 0)(lambda: body(*refs))
    else:
        operands = 2 * shards + 1
        kept = refs[:operands] + refs[operands + 5 :]
        pl.when(chip != 0)(lambda: body(*kept))


def block_state(first, taps, all_width, head_dim, groups, shards, own_columns, *refs):
    recv_refs, halos = refs[: shards - 1], refs[shards - 1 : 2 * shards - 1]
    rows_ref, tok = refs[2 * shards - 1 : 2 * shards + 1]
    xc_ref, bcc_ref, own_ref, own_d_ref, send_ref = refs[2 * shards + 1 : 2 * shards + 6]
    joined, scaled, full, full_d = refs[2 * shards + 6 :]
    position, sub = lax.axis_index("head"), lax.axis_index("sub")
    rows = own_columns.shape[0]
    width, bc_width = xc_ref.shape[1], bcc_ref.shape[1]
    group_width = width // groups
    piece = halos[0].shape[1]
    pieces = all_width // piece
    start, bc_start = first * group_width, first * 2 * STATE
    first_head = start // head_dim
    columns = slice(start, start + width)
    bc_columns = slice(all_width + bc_start, all_width + bc_start + bc_width)
    wx, bx = rows_ref[:taps, columns], rows_ref[taps : taps + 1, columns]
    wbc, bbc = rows_ref[:taps, bc_columns], rows_ref[taps : taps + 1, bc_columns]
    span = SPAN
    halo = halos[0][...].astype(F32)
    for j in range(1, shards):
        halo = jnp.where(lax.rem(position + 1, shards) == j, halos[j][...].astype(F32), halo)
    halo = jnp.where(lax.axis_index("seq") + sub == 0, 0.0, halo)
    for r in range(taps - 1):
        at = slice(EDGE - taps + 1 + r, EDGE - taps + 2 + r)
        for q in range(pieces):
            low, high = max(start, q * piece), min(start + width, (q + 1) * piece)
            if low < high:
                line = r * (pieces + 1) + q
                joined[at, low - start : high - start] = halo[
                    line : line + 1, low - q * piece : high - q * piece
                ]
        line = r * (pieces + 1) + pieces
        joined[at, width:] = halo[line : line + 1, bc_start : bc_start + bc_width]
    at = pl.multiple_of(EDGE + position * rows, EDGE)
    joined[pl.ds(at, rows), :width] = own_columns[:, columns].astype(F32)
    joined[pl.ds(at, rows), width:] = own_columns[:, bc_columns].astype(F32)
    for k, ref in enumerate(recv_refs):
        source = lax.rem(position + shards - 1 - k, shards)
        at = pl.multiple_of(EDGE + source * rows, EDGE)
        joined[pl.ds(at, rows), :] = ref[...].astype(F32)
    for j in range(bc_width // LANES):
        lanes = slice(j * LANES, (j + 1) * LANES)
        inner = slice(width + j * LANES, width + (j + 1) * LANES)
        bcc_ref[:, lanes] = conv_tile(joined, span, inner, wbc[:, lanes], bbc[:, lanes]).astype(BF16)
    to_end = tok[1]
    last = tok[2, span - EDGE :, :]
    lane = lane_index(span)
    lane_few = lane_index(EDGE)
    for j in range(width // LANES):
        lanes = slice(j * LANES, (j + 1) * LANES)
        xc = conv_tile(joined, span, lanes, wx[:, lanes], bx[:, lanes]).astype(BF16)
        xc_ref[:, lanes] = xc
        head = first_head + j * (LANES // head_dim)
        factor = widen_pair(to_end, head, head_dim, lane)
        scaled[:, lanes] = (factor * xc.astype(F32)).astype(BF16)
        full_d[:, lanes] = widen_pair(last, head, head_dim, lane_few)
    for g in range(groups):
        b_in = bcc_ref[:, g * 2 * STATE : g * 2 * STATE + STATE].astype(F32)
        lanes = slice(g * group_width, (g + 1) * group_width)
        full[:, lanes] = jnp.dot(b_in.T.astype(BF16), scaled[:, lanes], preferred_element_type=F32)
    half = width // 2
    mine = pl.ds(pl.multiple_of(sub * half, LANES), half)
    other = pl.ds(pl.multiple_of((1 - sub) * half, LANES), half)
    own_ref[...] = full[:, mine]
    own_d_ref[...] = full_d[EDGE - 1 :, mine]
    send_ref[:STATE, :] = full[:, other].astype(BF16)
    put_decay(send_ref, full_d[EDGE - 1 :, other])


def intra_kernel(first_head, head_dim, groups, xc_ref, bcc_ref, tok, heads_ref, by_head, y_ref):
    span, width = xc_ref.shape
    per_strip = LANES // head_dim
    lane = lane_index(span)
    group_width = width // groups
    causal = lax.broadcasted_iota(jnp.int32, (span, span), 0) >= lax.broadcasted_iota(
        jnp.int32, (span, span), 1
    )
    cum = tok[0]
    for g in range(groups):
        b_in = bcc_ref[:, g * 2 * STATE : g * 2 * STATE + STATE]
        c_out = bcc_ref[:, g * 2 * STATE + STATE : (g + 1) * 2 * STATE]
        inner = lax.dot_general(
            c_out, b_in, (((1,), (1,)), ((), ())), preferred_element_type=F32
        )
        inner = jnp.where(causal, inner, 0.0)
        for j in range(g * group_width // LANES, (g + 1) * group_width // LANES):
            lanes = slice(j * LANES, (j + 1) * LANES)
            xc = xc_ref[:, lanes]
            wide = xc.astype(F32)
            mixes, rights = [], []
            for k in range(per_strip):
                head = first_head + j * per_strip + k
                gap = cum[:, head : head + 1] - heads_ref[0, head : head + 1, :]
                weight = jnp.exp(jnp.minimum(gap, 0.0)) * heads_ref[1, head : head + 1, :]
                mixes.append((inner * weight).astype(BF16))
                own = (lane >= k * head_dim) & (lane < (k + 1) * head_dim)
                rights.append(jnp.where(own, wide, 0.0).astype(BF16))
            y = jnp.dot(
                jnp.concatenate(mixes, axis=1),
                jnp.concatenate(rights, axis=0),
                preferred_element_type=F32,
            )
            head = first_head + j * per_strip
            skip = widen_pair(by_head[2:3, :], head, head_dim, lane_index(1))
            y_ref[:, lanes] = (y + skip * wide).astype(y_ref.dtype)


def finish_kernel(first, gain_row, head_dim, groups, y_ref, bcc_ref, tok, mine, other, rows_ref, *refs):
    out_ref, carried, scratch, normed, sems = refs[-5:]
    span, width = y_ref.shape
    start = first * (width // groups)
    first_head = start // head_dim
    gain = rows_ref[gain_row : gain_row + 1, start : start + width]
    copies = []
    half = width // 2
    sub = lax.axis_index("sub")
    carried[:, pl.ds(pl.multiple_of(sub * half, LANES), half)] = mine[...]
    carried[:, pl.ds(pl.multiple_of((1 - sub) * half, LANES), half)] = other[...]
    lane = lane_index(span)
    group_width = width // groups
    decay = tok[2]
    for g in range(groups):
        c_out = bcc_ref[:, g * 2 * STATE + STATE : (g + 1) * 2 * STATE]
        lanes = slice(g * group_width, (g + 1) * group_width)
        scratch[...] = jnp.dot(c_out, carried[:, lanes], preferred_element_type=F32)
        squares = jnp.zeros((span, LANES), F32)
        for j in range(group_width // LANES):
            here = slice(j * LANES, (j + 1) * LANES)
            there = slice(g * group_width + j * LANES, g * group_width + (j + 1) * LANES)
            head = first_head + (g * group_width + j * LANES) // head_dim
            y = y_ref[:, there].astype(F32) + scratch[:, here] * widen_pair(decay, head, head_dim, lane)
            scratch[:, here] = y
            squares = squares + y * y
        mean = jnp.sum(squares, axis=1, keepdims=True) * (1.0 / group_width)
        factor = lax.rsqrt(mean + NORM_EPSILON)
        for j in range(group_width // LANES):
            here = slice(j * LANES, (j + 1) * LANES)
            there = slice(g * group_width + j * LANES, g * group_width + (j + 1) * LANES)
            normed[:, there] = (scratch[:, here] * factor * gain[:, there]).astype(BF16)
        target = slice(start + g * group_width, start + (g + 1) * group_width)
        copies.append(
            pltpu.make_async_copy(normed.at[:, lanes], out_ref.at[0, :, target], sems.at[g])
        )
        copies[-1].start()
    for copy in copies:
        copy.wait()


def copy_all(pairs, sems):
    copies = [pltpu.make_async_copy(a, b, sems.at[n]) for n, (a, b) in enumerate(pairs)]
    for copy in copies:
        copy.start()
    for copy in copies:
        copy.wait()


def columns_for(target, sources, out, parts):
    pairs = []
    column = 0
    for source, (stride, offset, count) in zip(sources, parts):
        start = pl.multiple_of(target * stride + offset, LANES)
        pairs.append((source.at[0, :, pl.ds(start, count)], out.at[:, pl.ds(column, count)]))
        column += count
    return pairs


def pack_kernel(shards, parts, x_ref, bc_ref, *refs):
    *outs, sems = refs
    position = lax.axis_index("head")
    pairs = []
    for k, out in enumerate(outs):
        target = lax.rem(position + k + 1, shards)
        pairs += columns_for(target, (x_ref, bc_ref), out, parts)
    copy_all(pairs, sems)


def tails_kernel(count, width, bc_width, x_ref, bc_ref, *refs):
    *outs, x_tail, bc_tail, sems = refs
    last = pl.ds(x_ref.shape[1] - EDGE, EDGE)
    copy_all([(x_ref.at[0, last, :], x_tail), (bc_ref.at[0, last, :], bc_tail)], sems)
    pieces = width // bc_width
    for j, out in enumerate(outs):
        k = (j + len(outs) - 1) % len(outs)
        lines = []
        for r in range(EDGE - count, EDGE):
            for q in range(pieces):
                at = k * width + q * bc_width
                lines.append(x_tail[:, at : at + bc_width].astype(F32)[r : r + 1, :])
            lines.append(bc_tail[:, k * bc_width : (k + 1) * bc_width].astype(F32)[r : r + 1, :])
        blank = jnp.zeros((out.shape[0] - len(lines), bc_width), F32)
        out[...] = jnp.concatenate(lines + [blank], axis=0).astype(BF16)


def put_decay(ref, decay):
    high = decay.astype(BF16).astype(F32)
    middle = (decay - high).astype(BF16).astype(F32)
    low = decay - high - middle
    row = lax.broadcasted_iota(jnp.int32, (EXTRA, decay.shape[1]), 0)
    parts = jnp.where(row == 0, high, 0.0)
    parts = jnp.where(row == 1, middle, parts)
    parts = jnp.where(row == 2, low, parts)
    ref[STATE:, :] = parts.astype(BF16)


def get_decay(ref):
    rows = ref[STATE:, :].astype(F32)
    return rows[0:1, :] + rows[1:2, :] + rows[2:3, :]


def get_state(ref):
    return ref[:STATE, :].astype(F32)


def join_kernel(own, own_d, got, decay, *totals):
    join_states(own, own_d, got, *totals)
    decay[...] = own_d[...] * get_decay(got)


def join_states(own, own_d, got, *totals):
    sub = lax.axis_index("sub")
    other_d = get_decay(got)
    step = own.shape[1] // len(totals)

    @pl.when(sub == 0)
    def _():
        for n, total in enumerate(totals):
            at = slice(n * step, (n + 1) * step)
            first, second = own[:, at], got[:STATE, at].astype(F32)
            total[...] = (other_d[:, at] * first + second).astype(BF16)

    @pl.when(sub != 0)
    def _():
        for n, total in enumerate(totals):
            at = slice(n * step, (n + 1) * step)
            first, second = got[:STATE, at].astype(F32), own[:, at]
            total[...] = (own_d[:, at] * first + second).astype(BF16)


def hop_kernel(n, total, decay, arrived, out):
    step = total.shape[1]
    here = decay[:, n * step : (n + 1) * step]
    out[...] = (here * arrived[...].astype(F32) + total[...].astype(F32)).astype(BF16)


def enter_blocks(own, own_d, got, final, mine, theirs):
    sub = lax.axis_index("sub")

    @pl.when(sub == 0)
    def _():
        mine[...] = final[...].astype(BF16)
        theirs[...] = (own_d[...] * final[...] + own[...]).astype(BF16)

    @pl.when(sub != 0)
    def _():
        theirs[...] = final[...].astype(BF16)
        mine[...] = (get_decay(got) * final[...] + get_state(got)).astype(BF16)


def pick_kernel(pieces, own, own_d, got, *refs):
    *arrived, mine, theirs, final = refs
    chip = lax.axis_index("seq")
    step = own.shape[1] // pieces

    @pl.when(chip == 0)
    def _():
        final[...] = jnp.zeros_like(final)

    for hop in range(len(arrived) // pieces):

        @pl.when(chip == hop + 1)
        def _():
            for n in range(pieces):
                final[:, n * step : (n + 1) * step] = arrived[hop * pieces + n][...].astype(F32)

    enter_blocks(own, own_d, got, final, mine, theirs)


def prep_kernel(
    shards, parts, x_ref, bc_ref, wx, bx, wbc, bbc, gain, offset, a_log, skip, *refs
):
    own_ref, rows_ref, heads_ref, *outs, sems = refs
    taps, width = wx.shape
    bc_width = wbc.shape[1]
    position = lax.axis_index("head")
    sources = (x_ref, bc_ref)
    pairs = []
    for n, out in enumerate(outs):
        target = lax.rem(position + 1 + n % (shards - 1), shards)
        pairs += columns_for(target, sources, out, parts[n // (shards - 1)])
    pairs += columns_for(position, sources, own_ref, ((width, 0, width), (bc_width, 0, bc_width)))
    copies = [pltpu.make_async_copy(a, b, sems.at[n]) for n, (a, b) in enumerate(pairs)]
    for copy in copies:
        copy.start()
    rows_ref[:taps, :width] = wx[...]
    rows_ref[taps : taps + 1, :width] = bx[...]
    rows_ref[taps + 1 : taps + 2, :width] = gain[...]
    rows_ref[:taps, width:] = wbc[...]
    rows_ref[taps : taps + 1, width:] = bbc[...]
    heads_ref[0:1, :] = offset[...]
    heads_ref[1:2, :] = a_log[...]
    heads_ref[2:3, :] = skip[...]
    for copy in copies:
        copy.wait()


def on_device(
    x_raw,
    bc_raw,
    dt_raw,
    conv_x_weight,
    conv_x_bias,
    conv_bc_weight,
    conv_bc_bias,
    stride_offset_per_head,
    a_log,
    skip_d,
    norm_gain,
):
    shards = lax.axis_size("head")
    chips = lax.axis_size("seq")
    rows = x_raw.shape[1]
    width = conv_x_weight.shape[1]
    bc_width = conv_bc_weight.shape[1]
    heads = a_log.shape[0]
    head_dim = width // heads
    groups = bc_width // (2 * STATE)
    group_width = width // groups
    plan = plan_of(groups)
    chunks = len(plan)
    counts = list(plan)
    firsts = [sum(counts[:c]) for c in range(chunks)]
    row = lambda a: a.reshape(1, a.shape[0])
    hbm = pl.BlockSpec(memory_space=pltpu.HBM)
    anywhere = pl.BlockSpec(memory_space=pl.ANY)
    vmem = pl.BlockSpec(memory_space=pltpu.VMEM)

    def call(kernel, operands, outs, scratch=(), specs=None, out_specs=None, aliases={}):
        return pl.pallas_call(
            kernel,
            in_specs=specs or [vmem] * len(operands),
            out_specs=out_specs or [vmem] * len(outs),
            scratch_shapes=list(scratch),
            out_shape=list(outs),
            input_output_aliases=aliases,
            compiler_params=pltpu.CompilerParams(vmem_limit_bytes=VMEM_LIMIT),
        )(*operands)

    def shift(k):
        return [(i, (i + k) % shards) for i in range(shards)]

    x_here = pltpu.with_memory_space_constraint(x_raw, pltpu.HBM)
    bc_here = pltpu.with_memory_space_constraint(bc_raw, pltpu.HBM)

    def parts_of(c):
        return (
            (width, firsts[c] * group_width, counts[c] * group_width),
            (bc_width, firsts[c] * 2 * STATE, counts[c] * 2 * STATE),
        )

    def payload(c):
        return pltpu.VMEM((rows, counts[c] * (group_width + 2 * STATE)), BF16)

    others = shards - 1
    packed = call(
        functools.partial(pack_kernel, shards, parts_of(0)),
        (x_here, bc_here),
        [payload(0)] * others,
        [pltpu.SemaphoreType.DMA((2 * others,))],
        specs=[hbm] * 2,
    )
    own_columns, rows_table, heads_table, *later = call(
        functools.partial(prep_kernel, shards, [parts_of(c) for c in range(1, chunks)]),
        (
            x_here,
            bc_here,
            conv_x_weight,
            row(conv_x_bias),
            conv_bc_weight,
            row(conv_bc_bias),
            row(norm_gain),
            row(stride_offset_per_head),
            row(a_log),
            row(skip_d),
        ),
        [
            pltpu.VMEM((rows, width + bc_width), BF16),
            pltpu.VMEM((8, width + bc_width), F32),
            pltpu.VMEM((8, heads), F32),
        ]
        + [payload(c) for c in range(1, chunks) for _ in range(others)],
        [pltpu.SemaphoreType.DMA((2 + 2 * others * (chunks - 1),))],
        specs=[hbm] * 2 + [vmem] * 8,
    )
    packed = list(packed) + later
    dt_recv = [lax.ppermute(dt_raw[0], "head", shift(k)) for k in range(1, shards)]
    recvs = [
        [lax.ppermute(packed[c * others + k - 1], "head", shift(k)) for k in range(1, shards)]
        for c in range(chunks)
    ]

    def following(j):
        return [
            ((b * shards + h) * 2 + t, (n // 2 * shards + (h + j) % shards) * 2 + n % 2)
            for b in range(chips)
            for t in range(2)
            for h in range(shards)
            for n in [(2 * b + t + 1) % (2 * chips)]
        ]

    taps = conv_x_weight.shape[0]
    lines = (taps - 1) * (width // bc_width + 1)
    tails = call(
        functools.partial(tails_kernel, taps - 1, width, bc_width),
        (x_here, bc_here),
        [pltpu.VMEM((-(-lines // 16) * 16, bc_width), BF16)] * shards,
        [
            pltpu.VMEM((EDGE, x_raw.shape[2]), BF16),
            pltpu.VMEM((EDGE, bc_raw.shape[2]), BF16),
            pltpu.SemaphoreType.DMA((2,)),
        ],
        specs=[hbm] * 2,
    )
    halos = [lax.ppermute(tails[j], ("seq", "head", "sub"), following(j)) for j in range(shards)]

    tok, by_head = call(
        functools.partial(tables_kernel, heads),
        (dt_raw, *dt_recv, heads_table),
        [pltpu.VMEM((3, SPAN, heads), F32), pltpu.VMEM((2, heads, SPAN), F32)],
        [pltpu.VMEM((SPAN, dt_raw.shape[2]), F32)],
    )

    def state(c, which, before=()):
        cw, cb = counts[c] * group_width, counts[c] * 2 * STATE
        half = cw // 2
        return call(
            functools.partial(
                state_kernel, which, firsts[c], taps, width, head_dim, counts[c], shards
            ),
            (own_columns, *recvs[c], *halos, rows_table, tok, *before),
            [
                pltpu.VMEM((SPAN, cw), BF16),
                pltpu.VMEM((SPAN, cb), BF16),
                pltpu.VMEM((STATE, half), F32),
                pltpu.VMEM((1, half), F32),
                pltpu.VMEM((STATE + EXTRA, half), BF16),
            ],
            [
                pltpu.VMEM((EDGE + SPAN, cw + cb), F32),
                pltpu.VMEM((SPAN, cw), BF16),
                pltpu.VMEM((STATE, cw), F32),
                pltpu.VMEM((EDGE, cw), F32),
            ],
            aliases={2 * shards + 2 + n: n for n in range(len(before))},
        )

    def lead(c):
        results = state(c, "first")
        own, own_d, send = results[2:]
        got = lax.ppermute(send, "sub", [(0, 1), (1, 0)])
        half = counts[c] * group_width // 2
        pieces = pieces_of(half, chips)
        totals = call(
            join_states, (own, own_d, got), [pltpu.VMEM((STATE, half // pieces), BF16)] * pieces
        )
        return totals, state(c, "rest", results)

    def carry(c, own, own_d, send, first_totals):
        half = counts[c] * group_width // 2
        pieces = pieces_of(half, chips)
        whole = pltpu.VMEM((STATE, half), F32)
        rounded = pltpu.VMEM((STATE, half), BF16)
        piece = pltpu.VMEM((STATE, half // pieces), BF16)
        got = lax.ppermute(send, "sub", [(0, 1), (1, 0)])
        decay, *totals = call(
            join_kernel, (own, own_d, got), [pltpu.VMEM((1, half), F32)] + [piece] * pieces
        )
        held = list(first_totals)
        arrived = []
        for hop in range(chips - 1):
            for n in range(pieces):
                arrived.append(lax.ppermute(held[n], "seq", [(hop, hop + 1)]))
                if hop < chips - 2:
                    (held[n],) = call(
                        functools.partial(hop_kernel, n), (totals[n], decay, arrived[-1]), [piece]
                    )
        mine, theirs = call(
            functools.partial(pick_kernel, pieces),
            (own, own_d, got, *arrived),
            [rounded] * 2,
            [whole],
        )
        return mine, lax.ppermute(theirs, "sub", [(0, 1), (1, 0)])

    def intra(c, xc, bcc):
        return call(
            functools.partial(
                intra_kernel, firsts[c] * group_width // head_dim, head_dim, counts[c]
            ),
            (xc, bcc, tok, by_head, heads_table),
            [pltpu.VMEM((SPAN, counts[c] * group_width), F32)],
        )[0]

    def finish(c, y, bcc, mine, theirs, out):
        before = [] if out is None else [out]
        cw = counts[c] * group_width
        return call(
            functools.partial(finish_kernel, firsts[c], taps + 1, head_dim, counts[c]),
            (y, bcc, tok, mine, theirs, rows_table, *before),
            [jax.ShapeDtypeStruct((1, SPAN, width), BF16)],
            [
                pltpu.VMEM((STATE, cw), BF16),
                pltpu.VMEM((SPAN, group_width), F32),
                pltpu.VMEM((SPAN, cw), BF16),
                pltpu.SemaphoreType.DMA((counts[c],)),
            ],
            specs=[vmem] * 6 + [anywhere] * len(before),
            out_specs=[anywhere],
            aliases={6: 0} if before else {},
        )[0]

    parts = []
    for c in range(chunks):
        first_totals, results = lead(c)
        xc, bcc, own, own_d, send = results
        mine, theirs = carry(c, own, own_d, send, first_totals)
        parts.append((intra(c, xc, bcc), bcc, mine, theirs))
    out = None
    for c in range(chunks):
        out = finish(c, *parts[c], out)
    return out


def pieces_of(half, chips):
    return PIECES if half % (PIECES * LANES) == 0 and chips <= 8 else 1


def solution(mesh):
    placed = (
        P(("groups", "seq", "sub"), "head", None),
        P(("groups", "seq", "sub"), "head", None),
        P(("groups", "seq", "sub"), "head", None),
        P(None, "head"),
        P("head"),
        P(None, "head"),
        P("head"),
        P("head"),
        P("head"),
        P("head"),
        P("head"),
    )
    return jax.shard_map(
        on_device,
        mesh=mesh,
        in_specs=placed,
        out_specs=P(("groups", "seq", "sub"), None, "head"),
        check_vma=False,
    )
```

```python
import functools

import jax
import jax.numpy as jnp
from jax import lax
from jax.experimental import pallas as pl
from jax.experimental.pallas import tpu as pltpu
from jax.sharding import PartitionSpec as P


STATE = 128
SPAN = 128
LANES = 128
EDGE = 8
EXTRA = 8
NORM_EPSILON = 1e-05
PIECES = 2
VMEM_LIMIT = 8 * 1024 * 1024


F32 = jnp.float32
BF16 = jnp.bfloat16


def plan_of(groups):
    return (groups - groups // 2, groups // 2) if groups > 1 else (groups,)


def silu(v):
    return v / (1.0 + jnp.exp(-v))


def widen_pair(table, head, head_dim, lanes):
    count = LANES // head_dim
    strip = jnp.broadcast_to(table[:, head : head + 1], (table.shape[0], LANES))
    for k in range(1, count):
        column = jnp.broadcast_to(table[:, head + k : head + k + 1], (table.shape[0], LANES))
        strip = jnp.where(lanes >= k * head_dim, column, strip)
    return strip


def lane_index(rows):
    return lax.broadcasted_iota(jnp.int32, (rows, LANES), 1)


def tables_kernel(heads, own_ref, *refs):
    *recv_refs, by_head, tok_ref, head_ref, raw = refs
    position = lax.axis_index("head")
    rows = own_ref.shape[1]
    shards = len(recv_refs) + 1
    raw[pl.ds(pl.multiple_of(position * rows, rows), rows), :] = own_ref[0].astype(F32)
    for k, ref in enumerate(recv_refs):
        source = lax.rem(position + shards - 1 - k, shards)
        raw[pl.ds(pl.multiple_of(source * rows, rows), rows), :] = ref[...].astype(F32)
    logits = raw[...]
    if shards > 1:
        total = logits.shape[1]
        logits = pltpu.roll(logits, lax.rem(total - position * heads, total), axis=1)
    v = logits[:, :heads] + by_head[0:1, :]
    dt = jnp.maximum(v, 0.0) + jnp.log1p(jnp.exp(-jnp.abs(v)))
    decay = -jnp.exp(by_head[1:2, :]) * dt
    span = decay.shape[0]
    lower = lax.broadcasted_iota(jnp.int32, (span, span), 0) >= lax.broadcasted_iota(
        jnp.int32, (span, span), 1
    )
    cum = jnp.dot(
        lower.astype(F32), decay, precision=lax.Precision.HIGHEST, preferred_element_type=F32
    )
    end = cum[span - 1 :, :]
    tok_ref[0] = cum
    tok_ref[1] = jnp.exp(end - cum) * dt
    tok_ref[2] = jnp.exp(cum)
    head_ref[0] = cum.T
    head_ref[1] = dt.T


def conv_tile(joined, rows, lanes, weight, bias):
    running = bias
    for tap in range(weight.shape[0]):
        start = EDGE - weight.shape[0] + 1 + tap
        running = running + weight[tap : tap + 1, :] * joined[pl.ds(start, rows), lanes]
    return silu(running)


def state_kernel(which, first, taps, all_width, head_dim, groups, shards, own_columns, *refs):
    chip = lax.axis_index("seq")
    body = functools.partial(
        block_state, first, taps, all_width, head_dim, groups, shards, own_columns
    )
    if which == "first":
        pl.when(chip == 0)(lambda: body(*refs))
    else:
        operands = 2 * shards + 1
        kept = refs[:operands] + refs[operands + 5 :]
        pl.when(chip != 0)(lambda: body(*kept))


def block_state(first, taps, all_width, head_dim, groups, shards, own_columns, *refs):
    recv_refs, halos = refs[: shards - 1], refs[shards - 1 : 2 * shards - 1]
    rows_ref, tok = refs[2 * shards - 1 : 2 * shards + 1]
    xc_ref, bcc_ref, own_ref, own_d_ref, send_ref = refs[2 * shards + 1 : 2 * shards + 6]
    joined, scaled, full, full_d = refs[2 * shards + 6 :]
    position, sub = lax.axis_index("head"), lax.axis_index("sub")
    rows = own_columns.shape[0]
    width, bc_width = xc_ref.shape[1], bcc_ref.shape[1]
    group_width = width // groups
    piece = halos[0].shape[1]
    pieces = all_width // piece
    start, bc_start = first * group_width, first * 2 * STATE
    first_head = start // head_dim
    columns = slice(start, start + width)
    bc_columns = slice(all_width + bc_start, all_width + bc_start + bc_width)
    wx, bx = rows_ref[:taps, columns], rows_ref[taps : taps + 1, columns]
    wbc, bbc = rows_ref[:taps, bc_columns], rows_ref[taps : taps + 1, bc_columns]
    span = SPAN
    halo = halos[0][...].astype(F32)
    for j in range(1, shards):
        halo = jnp.where(lax.rem(position + 1, shards) == j, halos[j][...].astype(F32), halo)
    halo = jnp.where(lax.axis_index("seq") + sub == 0, 0.0, halo)
    for r in range(taps - 1):
        at = slice(EDGE - taps + 1 + r, EDGE - taps + 2 + r)
        for q in range(pieces):
            low, high = max(start, q * piece), min(start + width, (q + 1) * piece)
            if low < high:
                line = r * (pieces + 1) + q
                joined[at, low - start : high - start] = halo[
                    line : line + 1, low - q * piece : high - q * piece
                ]
        line = r * (pieces + 1) + pieces
        joined[at, width:] = halo[line : line + 1, bc_start : bc_start + bc_width]
    at = pl.multiple_of(EDGE + position * rows, EDGE)
    joined[pl.ds(at, rows), :width] = own_columns[:, columns].astype(F32)
    joined[pl.ds(at, rows), width:] = own_columns[:, bc_columns].astype(F32)
    for k, ref in enumerate(recv_refs):
        source = lax.rem(position + shards - 1 - k, shards)
        at = pl.multiple_of(EDGE + source * rows, EDGE)
        joined[pl.ds(at, rows), :] = ref[...].astype(F32)
    for j in range(bc_width // LANES):
        lanes = slice(j * LANES, (j + 1) * LANES)
        inner = slice(width + j * LANES, width + (j + 1) * LANES)
        bcc_ref[:, lanes] = conv_tile(joined, span, inner, wbc[:, lanes], bbc[:, lanes]).astype(BF16)
    to_end = tok[1]
    last = tok[2, span - EDGE :, :]
    lane = lane_index(span)
    lane_few = lane_index(EDGE)
    for j in range(width // LANES):
        lanes = slice(j * LANES, (j + 1) * LANES)
        xc = conv_tile(joined, span, lanes, wx[:, lanes], bx[:, lanes]).astype(BF16)
        xc_ref[:, lanes] = xc
        head = first_head + j * (LANES // head_dim)
        factor = widen_pair(to_end, head, head_dim, lane)
        scaled[:, lanes] = (factor * xc.astype(F32)).astype(BF16)
        full_d[:, lanes] = widen_pair(last, head, head_dim, lane_few)
    for g in range(groups):
        b_in = bcc_ref[:, g * 2 * STATE : g * 2 * STATE + STATE].astype(F32)
        lanes = slice(g * group_width, (g + 1) * group_width)
        full[:, lanes] = jnp.dot(b_in.T.astype(BF16), scaled[:, lanes], preferred_element_type=F32)
    half = width // 2
    mine = pl.ds(pl.multiple_of(sub * half, LANES), half)
    other = pl.ds(pl.multiple_of((1 - sub) * half, LANES), half)
    own_ref[...] = full[:, mine]
    own_d_ref[...] = full_d[EDGE - 1 :, mine]
    send_ref[:STATE, :] = full[:, other].astype(BF16)
    put_decay(send_ref, full_d[EDGE - 1 :, other])


def intra_kernel(first_head, head_dim, groups, xc_ref, bcc_ref, tok, heads_ref, by_head, y_ref, wide_ref):
    span, width = xc_ref.shape
    per_strip = LANES // head_dim
    lane = lane_index(span)
    group_width = width // groups
    causal = lax.broadcasted_iota(jnp.int32, (span, span), 0) >= lax.broadcasted_iota(
        jnp.int32, (span, span), 1
    )
    cum = tok[0]
    for g in range(groups):
        b_in = bcc_ref[:, g * 2 * STATE : g * 2 * STATE + STATE]
        c_out = bcc_ref[:, g * 2 * STATE + STATE : (g + 1) * 2 * STATE]
        inner = lax.dot_general(
            c_out, b_in, (((1,), (1,)), ((), ())), preferred_element_type=F32
        )
        inner = jnp.where(causal, inner, 0.0)
        for j in range(g * group_width // LANES, (g + 1) * group_width // LANES):
            lanes = slice(j * LANES, (j + 1) * LANES)
            xc = xc_ref[:, lanes]
            wide = xc.astype(F32)
            mixes, rights = [], []
            for k in range(per_strip):
                head = first_head + j * per_strip + k
                gap = cum[:, head : head + 1] - heads_ref[0, head : head + 1, :]
                weight = jnp.exp(jnp.minimum(gap, 0.0)) * heads_ref[1, head : head + 1, :]
                mixes.append((inner * weight).astype(BF16))
                own = (lane >= k * head_dim) & (lane < (k + 1) * head_dim)
                rights.append(jnp.where(own, wide, 0.0).astype(BF16))
            y = jnp.dot(
                jnp.concatenate(mixes, axis=1),
                jnp.concatenate(rights, axis=0),
                preferred_element_type=F32,
            )
            head = first_head + j * per_strip
            skip = widen_pair(by_head[2:3, :], head, head_dim, lane_index(1))
            y_ref[:, lanes] = y + skip * wide
            wide_ref[:, lanes] = widen_pair(tok[2], head, head_dim, lane)


def finish_kernel(side, first, gain_row, groups, y_ref, wide_ref, bcc_ref, rows_ref, *refs):
    states, (scratch, normed, sems) = refs[: 2 if side == "both" else 1], refs[-3:]
    out_ref = refs[-5] if side == "both" else refs[-4]
    span, width = y_ref.shape
    group_width = width // groups
    half = width // 2
    sub = lax.axis_index("sub")
    if side == "both":
        carried, base, count = refs[-4], 0, groups
        carried[:, pl.ds(pl.multiple_of(sub * half, LANES), half)] = states[0][...]
        carried[:, pl.ds(pl.multiple_of((1 - sub) * half, LANES), half)] = states[1][...]
    else:
        carried, count = states[0], groups // 2
        base = (sub if side == "mine" else 1 - sub) * count

    def at(offset, size):
        return pl.ds(pl.multiple_of(offset, LANES), size)

    copies = []
    for g in range(count):
        group = base + g
        c_out = bcc_ref[:, at(group * 2 * STATE + STATE, STATE)]
        lanes = slice(g * group_width, (g + 1) * group_width)
        scratch[...] = jnp.dot(c_out, carried[:, lanes], preferred_element_type=F32)
        squares = jnp.zeros((span, LANES), F32)
        for j in range(group_width // LANES):
            here = slice(j * LANES, (j + 1) * LANES)
            there = at(group * group_width + j * LANES, LANES)
            y = y_ref[:, there] + scratch[:, here] * wide_ref[:, there]
            scratch[:, here] = y
            squares = squares + y * y
        mean = jnp.sum(squares, axis=1, keepdims=True) * (1.0 / group_width)
        factor = lax.rsqrt(mean + NORM_EPSILON)
        target = (first + group) * group_width
        for j in range(group_width // LANES):
            here = slice(j * LANES, (j + 1) * LANES)
            gain = rows_ref[gain_row : gain_row + 1, at(target + j * LANES, LANES)]
            inside = slice(g * group_width + j * LANES, g * group_width + (j + 1) * LANES)
            normed[:, inside] = (scratch[:, here] * factor * gain).astype(BF16)
        copies.append(
            pltpu.make_async_copy(
                normed.at[:, lanes], out_ref.at[0, :, at(target, group_width)], sems.at[g]
            )
        )
        copies[-1].start()
    for copy in copies:
        copy.wait()


def copy_all(pairs, sems):
    copies = [pltpu.make_async_copy(a, b, sems.at[n]) for n, (a, b) in enumerate(pairs)]
    for copy in copies:
        copy.start()
    for copy in copies:
        copy.wait()


def columns_for(target, sources, out, parts):
    pairs = []
    column = 0
    for source, (stride, offset, count) in zip(sources, parts):
        start = pl.multiple_of(target * stride + offset, LANES)
        pairs.append((source.at[0, :, pl.ds(start, count)], out.at[:, pl.ds(column, count)]))
        column += count
    return pairs


def pack_kernel(shards, parts, x_ref, bc_ref, *refs):
    *outs, sems = refs
    position = lax.axis_index("head")
    pairs = []
    for k, out in enumerate(outs):
        target = lax.rem(position + k + 1, shards)
        pairs += columns_for(target, (x_ref, bc_ref), out, parts)
    copy_all(pairs, sems)


def tails_kernel(count, width, bc_width, x_ref, bc_ref, *refs):
    *outs, x_tail, bc_tail, sems = refs
    last = pl.ds(x_ref.shape[1] - EDGE, EDGE)
    copy_all([(x_ref.at[0, last, :], x_tail), (bc_ref.at[0, last, :], bc_tail)], sems)
    pieces = width // bc_width
    for j, out in enumerate(outs):
        k = (j + len(outs) - 1) % len(outs)
        lines = []
        for r in range(EDGE - count, EDGE):
            for q in range(pieces):
                at = k * width + q * bc_width
                lines.append(x_tail[:, at : at + bc_width].astype(F32)[r : r + 1, :])
            lines.append(bc_tail[:, k * bc_width : (k + 1) * bc_width].astype(F32)[r : r + 1, :])
        blank = jnp.zeros((out.shape[0] - len(lines), bc_width), F32)
        out[...] = jnp.concatenate(lines + [blank], axis=0).astype(BF16)


def put_decay(ref, decay):
    high = decay.astype(BF16).astype(F32)
    middle = (decay - high).astype(BF16).astype(F32)
    low = decay - high - middle
    row = lax.broadcasted_iota(jnp.int32, (EXTRA, decay.shape[1]), 0)
    parts = jnp.where(row == 0, high, 0.0)
    parts = jnp.where(row == 1, middle, parts)
    parts = jnp.where(row == 2, low, parts)
    ref[STATE:, :] = parts.astype(BF16)


def get_decay(ref):
    rows = ref[STATE:, :].astype(F32)
    return rows[0:1, :] + rows[1:2, :] + rows[2:3, :]


def get_state(ref):
    return ref[:STATE, :].astype(F32)


def join_kernel(own, own_d, got, decay, *totals):
    join_states(own, own_d, got, *totals)
    decay[...] = own_d[...] * get_decay(got)


def join_states(own, own_d, got, *totals):
    sub = lax.axis_index("sub")
    other_d = get_decay(got)
    step = own.shape[1] // len(totals)

    @pl.when(sub == 0)
    def _():
        for n, total in enumerate(totals):
            at = slice(n * step, (n + 1) * step)
            first, second = own[:, at], got[:STATE, at].astype(F32)
            total[...] = (other_d[:, at] * first + second).astype(BF16)

    @pl.when(sub != 0)
    def _():
        for n, total in enumerate(totals):
            at = slice(n * step, (n + 1) * step)
            first, second = got[:STATE, at].astype(F32), own[:, at]
            total[...] = (own_d[:, at] * first + second).astype(BF16)


def hop_kernel(n, total, decay, arrived, out):
    step = total.shape[1]
    here = decay[:, n * step : (n + 1) * step]
    out[...] = (here * arrived[...].astype(F32) + total[...].astype(F32)).astype(BF16)


def enter_blocks(own, own_d, got, final, mine, theirs):
    sub = lax.axis_index("sub")

    @pl.when(sub == 0)
    def _():
        mine[...] = final[...].astype(BF16)
        theirs[...] = (own_d[...] * final[...] + own[...]).astype(BF16)

    @pl.when(sub != 0)
    def _():
        theirs[...] = final[...].astype(BF16)
        mine[...] = (get_decay(got) * final[...] + get_state(got)).astype(BF16)


def pick_kernel(pieces, own, own_d, got, *refs):
    *arrived, mine, theirs, final = refs
    chip = lax.axis_index("seq")
    step = own.shape[1] // pieces

    @pl.when(chip == 0)
    def _():
        final[...] = jnp.zeros_like(final)

    for hop in range(len(arrived) // pieces):

        @pl.when(chip == hop + 1)
        def _():
            for n in range(pieces):
                final[:, n * step : (n + 1) * step] = arrived[hop * pieces + n][...].astype(F32)

    enter_blocks(own, own_d, got, final, mine, theirs)


def prep_kernel(
    shards, parts, x_ref, bc_ref, wx, bx, wbc, bbc, gain, offset, a_log, skip, *refs
):
    own_ref, rows_ref, heads_ref, *outs, sems = refs
    taps, width = wx.shape
    bc_width = wbc.shape[1]
    position = lax.axis_index("head")
    sources = (x_ref, bc_ref)
    pairs = []
    for n, out in enumerate(outs):
        target = lax.rem(position + 1 + n % (shards - 1), shards)
        pairs += columns_for(target, sources, out, parts[n // (shards - 1)])
    pairs += columns_for(position, sources, own_ref, ((width, 0, width), (bc_width, 0, bc_width)))
    copies = [pltpu.make_async_copy(a, b, sems.at[n]) for n, (a, b) in enumerate(pairs)]
    for copy in copies:
        copy.start()
    rows_ref[:taps, :width] = wx[...]
    rows_ref[taps : taps + 1, :width] = bx[...]
    rows_ref[taps + 1 : taps + 2, :width] = gain[...]
    rows_ref[:taps, width:] = wbc[...]
    rows_ref[taps : taps + 1, width:] = bbc[...]
    heads_ref[0:1, :] = offset[...]
    heads_ref[1:2, :] = a_log[...]
    heads_ref[2:3, :] = skip[...]
    for copy in copies:
        copy.wait()


def on_device(
    x_raw,
    bc_raw,
    dt_raw,
    conv_x_weight,
    conv_x_bias,
    conv_bc_weight,
    conv_bc_bias,
    stride_offset_per_head,
    a_log,
    skip_d,
    norm_gain,
):
    shards = lax.axis_size("head")
    chips = lax.axis_size("seq")
    rows = x_raw.shape[1]
    width = conv_x_weight.shape[1]
    bc_width = conv_bc_weight.shape[1]
    heads = a_log.shape[0]
    head_dim = width // heads
    groups = bc_width // (2 * STATE)
    group_width = width // groups
    plan = plan_of(groups)
    chunks = len(plan)
    counts = list(plan)
    firsts = [sum(counts[:c]) for c in range(chunks)]
    row = lambda a: a.reshape(1, a.shape[0])
    hbm = pl.BlockSpec(memory_space=pltpu.HBM)
    anywhere = pl.BlockSpec(memory_space=pl.ANY)
    vmem = pl.BlockSpec(memory_space=pltpu.VMEM)

    def call(kernel, operands, outs, scratch=(), specs=None, out_specs=None, aliases={}):
        return pl.pallas_call(
            kernel,
            in_specs=specs or [vmem] * len(operands),
            out_specs=out_specs or [vmem] * len(outs),
            scratch_shapes=list(scratch),
            out_shape=list(outs),
            input_output_aliases=aliases,
            compiler_params=pltpu.CompilerParams(vmem_limit_bytes=VMEM_LIMIT),
        )(*operands)

    def shift(k):
        return [(i, (i + k) % shards) for i in range(shards)]

    x_here = pltpu.with_memory_space_constraint(x_raw, pltpu.HBM)
    bc_here = pltpu.with_memory_space_constraint(bc_raw, pltpu.HBM)

    def parts_of(c):
        return (
            (width, firsts[c] * group_width, counts[c] * group_width),
            (bc_width, firsts[c] * 2 * STATE, counts[c] * 2 * STATE),
        )

    def payload(c):
        return pltpu.VMEM((rows, counts[c] * (group_width + 2 * STATE)), BF16)

    others = shards - 1
    packed = call(
        functools.partial(pack_kernel, shards, parts_of(0)),
        (x_here, bc_here),
        [payload(0)] * others,
        [pltpu.SemaphoreType.DMA((2 * others,))],
        specs=[hbm] * 2,
    )
    own_columns, rows_table, heads_table, *later = call(
        functools.partial(prep_kernel, shards, [parts_of(c) for c in range(1, chunks)]),
        (
            x_here,
            bc_here,
            conv_x_weight,
            row(conv_x_bias),
            conv_bc_weight,
            row(conv_bc_bias),
            row(norm_gain),
            row(stride_offset_per_head),
            row(a_log),
            row(skip_d),
        ),
        [
            pltpu.VMEM((rows, width + bc_width), BF16),
            pltpu.VMEM((8, width + bc_width), F32),
            pltpu.VMEM((8, heads), F32),
        ]
        + [payload(c) for c in range(1, chunks) for _ in range(others)],
        [pltpu.SemaphoreType.DMA((2 + 2 * others * (chunks - 1),))],
        specs=[hbm] * 2 + [vmem] * 8,
    )
    packed = list(packed) + later
    dt_recv = [lax.ppermute(dt_raw[0], "head", shift(k)) for k in range(1, shards)]
    recvs = [
        [lax.ppermute(packed[c * others + k - 1], "head", shift(k)) for k in range(1, shards)]
        for c in range(chunks)
    ]

    def following(j):
        return [
            ((b * shards + h) * 2 + t, (n // 2 * shards + (h + j) % shards) * 2 + n % 2)
            for b in range(chips)
            for t in range(2)
            for h in range(shards)
            for n in [(2 * b + t + 1) % (2 * chips)]
        ]

    taps = conv_x_weight.shape[0]
    lines = (taps - 1) * (width // bc_width + 1)
    tails = call(
        functools.partial(tails_kernel, taps - 1, width, bc_width),
        (x_here, bc_here),
        [pltpu.VMEM((-(-lines // 16) * 16, bc_width), BF16)] * shards,
        [
            pltpu.VMEM((EDGE, x_raw.shape[2]), BF16),
            pltpu.VMEM((EDGE, bc_raw.shape[2]), BF16),
            pltpu.SemaphoreType.DMA((2,)),
        ],
        specs=[hbm] * 2,
    )
    halos = [lax.ppermute(tails[j], ("seq", "head", "sub"), following(j)) for j in range(shards)]

    tok, by_head = call(
        functools.partial(tables_kernel, heads),
        (dt_raw, *dt_recv, heads_table),
        [pltpu.VMEM((3, SPAN, heads), F32), pltpu.VMEM((2, heads, SPAN), F32)],
        [pltpu.VMEM((SPAN, dt_raw.shape[2]), F32)],
    )

    def state(c, which, before=()):
        cw, cb = counts[c] * group_width, counts[c] * 2 * STATE
        half = cw // 2
        return call(
            functools.partial(
                state_kernel, which, firsts[c], taps, width, head_dim, counts[c], shards
            ),
            (own_columns, *recvs[c], *halos, rows_table, tok, *before),
            [
                pltpu.VMEM((SPAN, cw), BF16),
                pltpu.VMEM((SPAN, cb), BF16),
                pltpu.VMEM((STATE, half), F32),
                pltpu.VMEM((1, half), F32),
                pltpu.VMEM((STATE + EXTRA, half), BF16),
            ],
            [
                pltpu.VMEM((EDGE + SPAN, cw + cb), F32),
                pltpu.VMEM((SPAN, cw), BF16),
                pltpu.VMEM((STATE, cw), F32),
                pltpu.VMEM((EDGE, cw), F32),
            ],
            aliases={2 * shards + 2 + n: n for n in range(len(before))},
        )

    def lead(c):
        results = state(c, "first")
        own, own_d, send = results[2:]
        got = lax.ppermute(send, "sub", [(0, 1), (1, 0)])
        half = counts[c] * group_width // 2
        pieces = pieces_of(half, chips)
        totals = call(
            join_states, (own, own_d, got), [pltpu.VMEM((STATE, half // pieces), BF16)] * pieces
        )
        return totals, state(c, "rest", results)

    def carry(c, own, own_d, send, first_totals):
        half = counts[c] * group_width // 2
        pieces = pieces_of(half, chips)
        whole = pltpu.VMEM((STATE, half), F32)
        rounded = pltpu.VMEM((STATE, half), BF16)
        piece = pltpu.VMEM((STATE, half // pieces), BF16)
        got = lax.ppermute(send, "sub", [(0, 1), (1, 0)])
        decay, *totals = call(
            join_kernel, (own, own_d, got), [pltpu.VMEM((1, half), F32)] + [piece] * pieces
        )
        held = list(first_totals)
        arrived = []
        for hop in range(chips - 1):
            for n in range(pieces):
                arrived.append(lax.ppermute(held[n], "seq", [(hop, hop + 1)]))
                if hop < chips - 2:
                    (held[n],) = call(
                        functools.partial(hop_kernel, n), (totals[n], decay, arrived[-1]), [piece]
                    )
        mine, theirs = call(
            functools.partial(pick_kernel, pieces),
            (own, own_d, got, *arrived),
            [rounded] * 2,
            [whole],
        )
        return mine, lax.ppermute(theirs, "sub", [(0, 1), (1, 0)])

    def intra(c, xc, bcc):
        return call(
            functools.partial(
                intra_kernel, firsts[c] * group_width // head_dim, head_dim, counts[c]
            ),
            (xc, bcc, tok, by_head, heads_table),
            [pltpu.VMEM((SPAN, counts[c] * group_width), F32)] * 2,
        )

    def finish(c, side, y, wide, bcc, states, out):
        before = [] if out is None else [out]
        count = counts[c] if side == "both" else counts[c] // 2
        held = [pltpu.VMEM((STATE, counts[c] * group_width), BF16)] if side == "both" else []
        return call(
            functools.partial(finish_kernel, side, firsts[c], taps + 1, counts[c]),
            (y, wide, bcc, rows_table, *states, *before),
            [jax.ShapeDtypeStruct((1, SPAN, width), BF16)],
            held
            + [
                pltpu.VMEM((SPAN, group_width), F32),
                pltpu.VMEM((SPAN, count * group_width), BF16),
                pltpu.SemaphoreType.DMA((count,)),
            ],
            specs=[vmem] * (4 + len(states)) + [anywhere] * len(before),
            out_specs=[anywhere],
            aliases={4 + len(states): 0} if before else {},
        )[0]

    parts = []
    for c in range(chunks):
        first_totals, results = lead(c)
        xc, bcc, own, own_d, send = results
        mine, theirs = carry(c, own, own_d, send, first_totals)
        parts.append(((*intra(c, xc, bcc), bcc), mine, theirs))
    out = None
    for c in range(chunks):
        local, mine, theirs = parts[c]
        if counts[c] % 2 == 0:
            out = finish(c, "mine", *local, (mine,), out)
            out = finish(c, "other", *local, (theirs,), out)
        else:
            out = finish(c, "both", *local, (mine, theirs), out)
    return out


def pieces_of(half, chips):
    return PIECES if half % (PIECES * LANES) == 0 and chips <= 8 else 1


def solution(mesh):
    placed = (
        P(("groups", "seq", "sub"), "head", None),
        P(("groups", "seq", "sub"), "head", None),
        P(("groups", "seq", "sub"), "head", None),
        P(None, "head"),
        P("head"),
        P(None, "head"),
        P("head"),
        P("head"),
        P("head"),
        P("head"),
        P("head"),
    )
    return jax.shard_map(
        on_device,
        mesh=mesh,
        in_specs=placed,
        out_specs=P(("groups", "seq", "sub"), None, "head"),
        check_vma=False,
    )
```
